512 devices in a mesh: band: 128 (over z, y, core), batch: 4 (over x).
Axes of the slice: x: 4, y: 4, z: 16, core: 2. Of those that a mesh axis runs over, the one named last changes fastest.
Arguments:
- tiles: bfloat16 [128, 128, 128, 128], P('band'), may hold values from -256 to 256, as said below
- tile_row: int32 [128, 128], P('band'), may hold values from 0 to 3, as said below
- tile_col: int32 [128, 128], P('band'), may hold values from 0 to 255, as said below
- tile_count: int32 [128], P('band'), may hold values from 80 to 128, as said below
- cost: float32 [8, 32768], P('batch', 'band'), may hold values from -6 to 6
- bound_vec: float32 [65536], P('band'), may hold values from -6 to 6
- x_start: float32 [8, 32768], P('batch', 'band'), may hold values from 0 to 1
- y_start: float32 [8, 65536], P('batch', 'band'), may hold values from 0 to 1
Outputs:
- x_out: float32 [8, 32768], P('batch', 'band')
- y_out: float32 [8, 65536], P('batch', 'band')
The draws below stay inside these ranges and needn't reach their ends.
Inputs may be any that keep to these rules, and one draw needn't show every extreme that they name: `tile_row`: within a band, tiles 0 to 3 lie in row blocks 0 to 3 in order. `tile_col`: the owner of column block k is band k // 2. Among a band's live tiles at most 2 have one owner, and the tiles of one owner stand in a row; tiles 0 to 1 of band b lie in column blocks b * 2 + t, so each band gives exactly 2 tiles to its own owner and every row block and column block holds a live tile. `tile_count`: one band in every draw is full. `tiles`: every entry has magnitude 0.1 or more.
All inputs are finite; a program needn't handle non-finite values.
Results may differ from the reference program's by a relative error of at most 0.0003.
Values sent between devices are 32-bit elements; how exact they have to be, the bound alone decides.
A program may use at most 64 MiB of HBM per device.

```python
import math
import jax
import jax.numpy as jnp
from jax import lax

TILE = 128
TILES = 128
ROWBLK = 4
COLBLK = 2
COSTS = 8
BANDS = 128
CAPACITY = 2
NROW = 65536
NCOL = 32768


def pattern(key):
    base = jax.random.fold_in(key, 7)
    band_keys = jax.random.split(base, BANDS)

    def one_band(band_key, band):
        key_perm, key_counts, key_cols, key_rows = jax.random.split(band_key, 4)
        shuffled = jax.random.permutation(key_perm, BANDS).astype(jnp.int32)
        where_band = jnp.argmax(shuffled == band)
        owners = shuffled.at[where_band].set(shuffled[0]).at[0].set(band)
        lowest = max(1, CAPACITY // 2)
        group_sizes = jax.random.randint(key_counts, (BANDS,), lowest, CAPACITY + 1).astype(jnp.int32).at[0].set(CAPACITY)
        starts = jnp.cumsum(group_sizes) - group_sizes
        indices = jnp.arange(TILES, dtype=jnp.int32)
        group = (jnp.sum((starts[None, :] <= indices[:, None]).astype(jnp.int32), axis=1) - 1).astype(jnp.int32)
        owner_of = owners[group]
        tile_cols = owner_of * COLBLK + jax.random.randint(key_cols, (TILES,), 0, COLBLK).astype(jnp.int32)
        tile_cols = jnp.where(indices < COLBLK, band * COLBLK + indices, tile_cols)
        tile_rows = jax.random.randint(key_rows, (TILES,), 0, ROWBLK).astype(jnp.int32)
        tile_rows = jnp.where(indices < ROWBLK, indices, tile_rows)
        return (tile_rows, tile_cols)
    tile_rows, tile_cols = jax.vmap(one_band)(band_keys, jnp.arange(BANDS, dtype=jnp.int32))
    key_live, key_full = jax.random.split(jax.random.fold_in(base, 11))
    lowest_count = max(5 * TILES // 8, ROWBLK, COLBLK)
    live_count = jax.random.randint(key_live, (BANDS,), lowest_count, TILES + 1).astype(jnp.int32)
    full_band = jax.random.randint(key_full, (), 0, BANDS)
    live_count = live_count.at[full_band].set(TILES)
    return (tile_rows, tile_cols, live_count)


def draw_tile_row(key, part):
    return pattern(key)[0]


def draw_tile_col(key, part):
    return pattern(key)[1]


def draw_tile_count(key, part):
    return pattern(key)[2]


def draw_tiles(key, part):
    key_sign, key_mag, key_row, key_col = jax.random.split(key, 4)
    shape = (BANDS, TILES, TILE, TILE)
    signs = jnp.where(jax.random.uniform(key_sign, shape) < 0.5, -1.0, 1.0)
    magnitude = jnp.exp(jax.random.uniform(key_mag, shape, jnp.float32, math.log(0.1), 0.0))
    spread = math.log(10.0)
    row_factor = jnp.exp(jax.random.uniform(key_row, (BANDS, TILES, TILE, 1), jnp.float32, 0.0, spread))
    col_factor = jnp.exp(jax.random.uniform(key_col, (BANDS, TILES, 1, TILE), jnp.float32, 0.0, spread))
    return (signs * magnitude * row_factor * col_factor).astype(jnp.bfloat16)


def block_scale(key, dims, pieces, smallest, high):
    level, own = 1.0, jax.random.fold_in(key, 6)
    for position, blocks in pieces:
        draws = jnp.exp(jax.random.uniform(jax.random.fold_in(own, position), (blocks,), jnp.float32, smallest / len(pieces), high / len(pieces)))
        level = level * jnp.repeat(draws, dims[position] // blocks).reshape([-1 if axis == position else 1 for axis in range(len(dims))])
    return level


def noise(stream_key, dims, scale, reach, pieces=(), kind=jnp.bfloat16):
    entries = jax.random.normal(stream_key, dims, jnp.float32) * scale
    if len(pieces) > 0:
        entries = block_scale(stream_key, dims, pieces, -0.22, 0.18) * entries
    return jnp.clip(entries, min=-reach, max=reach).astype(kind)


def setup_inputs(seed: int = 0) -> dict:
    arg_keys = jax.random.split(jax.random.key(seed), 9)
    return {
        "tiles": draw_tiles(jax.random.fold_in(arg_keys[8], 71), 0),
        "tile_row": draw_tile_row(jax.random.fold_in(arg_keys[8], 71), 0),
        "tile_col": draw_tile_col(jax.random.fold_in(arg_keys[8], 71), 0),
        "tile_count": draw_tile_count(jax.random.fold_in(arg_keys[8], 71), 0),
        "cost": noise(arg_keys[4], (COSTS, NCOL), 1.0, 6.0, ((0, 4), (1, 128)), jnp.float32),
        "bound_vec": noise(arg_keys[5], (NROW,), 1.0, 6.0, ((0, 128),), jnp.float32),
        "x_start": jnp.clip(1.0 * jax.random.uniform(arg_keys[6], (COSTS, NCOL), jnp.float32) ** block_scale(arg_keys[6], (COSTS, NCOL), ((0, 4), (1, 128)), -0.2, 0.2), 0.0, 1.0),
        "y_start": jnp.clip(1.0 * jax.random.uniform(arg_keys[7], (COSTS, NROW), jnp.float32) ** block_scale(arg_keys[7], (COSTS, NROW), ((0, 4), (1, 128)), -0.2, 0.2), 0.0, 1.0),
    }


step_size = 0.0625
high = lax.Precision.HIGHEST

def reference(tiles, tile_row, tile_col, tile_count, cost, bound_vec, x_start, y_start):
    band_count = tiles.shape[0]
    tile_edge = tiles.shape[2]
    indices = jnp.arange(tiles.shape[1], dtype=jnp.int32)
    live = indices[None, :] < tile_count[:, None]
    rowsel = (tile_row[:, None, :] == jnp.arange(ROWBLK, dtype=jnp.int32)[None, :, None]) & live[:, None, :]

    def row_peaks(args):
        block, select, alive = args
        magnitude = jnp.abs(block.astype(jnp.float32))
        row_max = jnp.where(alive[:, None], lax.optimization_barrier(jnp.max(magnitude, axis=2)), 0.0)
        return lax.optimization_barrier(jnp.max(jnp.where(select[:, :, None], row_max[None], 0.0), axis=1))
    rscale = lax.rsqrt(lax.map(row_peaks, (tiles, rowsel, live)))

    def col_peaks(args):
        block, tile_rows, alive, scales = args
        spread = scales[tile_rows]
        peak = lax.optimization_barrier(jnp.max(jnp.abs(block.astype(jnp.float32)) * spread[:, :, None], axis=1))
        return jnp.where(alive[:, None], peak, 0.0)
    col_tile = lax.map(col_peaks, (tiles, tile_row, live, rscale))
    col_max = jnp.zeros((COLBLK * band_count, tile_edge), jnp.float32).at[tile_col.reshape(-1)].max(col_tile.reshape(-1, tile_edge))
    cscale = lax.rsqrt(col_max).reshape(-1)
    rflat = rscale.reshape(-1)

    def forward(vec):
        scaled = (vec * cscale).reshape(vec.shape[0], COLBLK * band_count, tile_edge)

        def one_band(args):
            block, tile_cols, alive, select = args
            picked = jnp.take(scaled, tile_cols, axis=1)
            product = jnp.einsum('tij,ktj->tki', block.astype(jnp.float32), picked, precision=high)
            product = jnp.where(alive[:, None, None], product, 0.0)
            return jnp.einsum('rt,tki->kri', select.astype(jnp.float32), product, precision=high)
        result = lax.map(one_band, (tiles, tile_col, live, rowsel))
        return jnp.transpose(result, (1, 0, 2, 3)).reshape(vec.shape[0], -1) * rflat

    def adjoint(vec):
        weighted = (vec * rflat).reshape(vec.shape[0], band_count, ROWBLK, tile_edge)

        def one_band(total, args):
            block, band_w, tile_cols, alive, select = args
            spread = jnp.einsum('rt,kri->tki', select.astype(jnp.float32), band_w, precision=high)
            partial_value = jnp.einsum('tij,tki->ktj', block.astype(jnp.float32), spread, precision=high)
            partial_value = jnp.where(alive[None, :, None], partial_value, 0.0)
            return (total.at[:, tile_cols].add(partial_value), None)
        start = jnp.zeros((vec.shape[0], COLBLK * band_count, tile_edge), jnp.float32)
        total, _unused = lax.scan(one_band, start, (tiles, jnp.moveaxis(weighted, 1, 0), tile_col, live, rowsel))
        return total.reshape(vec.shape[0], -1) * cscale
    scost = cost * cscale
    sbound = bound_vec * rflat
    primal_one = jnp.maximum(0.0, x_start - step_size * (scost - adjoint(y_start)))
    dual_one = jnp.maximum(0.0, y_start + step_size * (sbound - forward(2.0 * primal_one - x_start)))
    primal_step = lax.optimization_barrier(jnp.sum((primal_one - x_start) ** 2, axis=1, keepdims=True))
    dual_step = lax.optimization_barrier(jnp.sum((dual_one - y_start) ** 2, axis=1, keepdims=True))
    weight_ratio = jnp.sqrt((dual_step + 1e-06) / (primal_step + 1e-06))
    primal_two = jnp.maximum(0.0, primal_one - step_size / weight_ratio * (scost - adjoint(dual_one)))
    dual_two = jnp.maximum(0.0, dual_one + step_size * weight_ratio * (sbound - forward(2.0 * primal_two - primal_one)))
    return (primal_two, dual_two)
```

```python
import functools

import jax
import jax.numpy as jnp
from jax import lax
from jax.experimental import pallas as pl
from jax.experimental.pallas import tpu as pltpu
from jax.sharding import PartitionSpec as P

ROWBLK = 4
COLBLK = 2
PLANE = 8
UNROLL = 8

step_size = 0.0625
MESH = pl.DeviceIdType.MESH
F32 = jnp.float32
BF16 = jnp.bfloat16


def rows8():
    return lax.broadcasted_iota(jnp.int32, (8, 128), 0)


def split_parts(value):
    high = value.astype(BF16).astype(F32)
    return jnp.concatenate([high, value - high], axis=0).astype(BF16)


def place_of(owner, depth):
    return (owner % PLANE) * depth + owner // PLANE


def dual_rows(ref):
    return jnp.concatenate(
        [ref[k : k + 1, r * 128 : (r + 1) * 128] for k in range(2) for r in range(ROWBLK)], axis=0
    )


def bound_rows(ref):
    rows = [ref[0:1, r * 128 : (r + 1) * 128] for r in range(ROWBLK)]
    return jnp.concatenate(rows + rows, axis=0)


def fill_weights(weighted, table):
    row = rows8()
    for r in range(ROWBLK):
        first = jnp.broadcast_to(weighted[r : r + 1], (8, 128))
        second = jnp.broadcast_to(weighted[ROWBLK + r : ROWBLK + r + 1], (8, 128))
        for c in range(COLBLK):
            entry = jnp.where(row == 2 * c, first, jnp.where(row == 2 * c + 1, second, 0.0))
            table[r * COLBLK + c] = split_parts(entry)
    table[ROWBLK * COLBLK] = jnp.zeros((16, 128), BF16)


def forward_rows(tiles, tile_row, tile_col, count, gathered):
    ntile = tiles.shape[1]
    depth = gathered.shape[0] // (PLANE * COLBLK)
    row = rows8()

    def body(step, acc):
        for u in range(UNROLL):
            t = step * UNROLL + u
            r = jnp.where(t < count, tile_row[0, t], ROWBLK)
            col = tile_col[0, t]
            pair = gathered[place_of(col // COLBLK, depth) * COLBLK + col % COLBLK]
            value = jnp.where(
                row < ROWBLK,
                jnp.broadcast_to(pair[0:1], (8, 128)),
                jnp.broadcast_to(pair[1:2], (8, 128)),
            )
            value = jnp.where(row % ROWBLK == r, value, 0.0)
            acc = acc + lax.dot_general(
                split_parts(value),
                tiles[0, t],
                (((1,), (1,)), ((), ())),
                preferred_element_type=F32,
            )
        return acc

    acc = lax.fori_loop(0, ntile // UNROLL, body, jnp.zeros((16, 128), F32))
    return acc[0:8] + acc[8:16]


def scale_kernel(
    tiles, tile_row, tile_col, tile_count, y_start, outgoing, rscale, peaks, spread, table
):
    ntile = tiles.shape[1]
    depth = outgoing.shape[0] // PLANE
    count = tile_count[0]
    row = rows8()
    peaks[...] = jnp.zeros_like(peaks)

    def peak_body(step, carry):
        for u in range(UNROLL):
            t = step * UNROLL + u
            r = jnp.where(t < count, tile_row[0, t], ROWBLK)
            peaks[r] = jnp.maximum(peaks[r], jnp.abs(tiles[0, t]))
        return carry

    lax.fori_loop(0, ntile // UNROLL, peak_body, 0)
    rows = []
    for r in range(ROWBLK):
        peak = jnp.max(peaks[r].astype(F32), axis=1, keepdims=True)
        scale = jnp.broadcast_to(lax.rsqrt(peak), (128, 128))
        spread[r] = scale
        rows.append(jnp.transpose(scale)[0:1])
    spread[ROWBLK] = jnp.zeros((128, 128), F32)
    scales = jnp.concatenate(rows + rows, axis=0)
    rscale[...] = scales
    fill_weights(dual_rows(y_start) * scales, table)
    outgoing[...] = jnp.zeros_like(outgoing)

    def body(step, carry):
        for u in range(UNROLL):
            t = step * UNROLL + u
            r = jnp.where(t < count, tile_row[0, t], ROWBLK)
            col = tile_col[0, t]
            part = col % COLBLK
            place = place_of(col // COLBLK, depth)
            block = tiles[0, t]
            peak = jnp.max(jnp.abs(block.astype(F32)) * spread[r], axis=0, keepdims=True)
            peak = jnp.where(row == 4 + part, jnp.broadcast_to(peak, (8, 128)), 0.0)
            weights = table[jnp.minimum(r * COLBLK + part, ROWBLK * COLBLK)]
            product = jnp.dot(weights, block, preferred_element_type=F32)
            held = outgoing[place]
            outgoing[place] = jnp.where(
                row < 4, held + product[0:8] + product[8:16], jnp.maximum(held, peak)
            )
        return carry

    lax.fori_loop(0, ntile // UNROLL, body, 0)


def dual_kernel(
    tiles,
    tile_row,
    tile_col,
    tile_count,
    gathered,
    y_start,
    bound_vec,
    rscale,
    primal_step,
    outgoing,
    dual_out,
    table,
):
    ntile = tiles.shape[1]
    depth = outgoing.shape[0] // PLANE
    count = tile_count[0]
    row = rows8()
    scales = rscale[...]
    start = dual_rows(y_start)
    product = forward_rows(tiles, tile_row, tile_col, count, gathered) * scales
    dual = jnp.maximum(0.0, start + step_size * (bound_rows(bound_vec) * scales - product))
    dual_out[...] = dual
    move = (dual - start) ** 2
    first = jnp.sum(move[0:4], axis=0, keepdims=True)
    second = jnp.sum(move[4:8], axis=0, keepdims=True)
    steps = jnp.where(
        row == 6,
        jnp.broadcast_to(first, (8, 128)),
        jnp.where(row == 7, jnp.broadcast_to(second, (8, 128)), primal_step[...]),
    )
    fill_weights(dual * scales, table)
    outgoing[...] = jnp.broadcast_to(steps[None], outgoing.shape)

    def body(step, carry):
        for u in range(UNROLL):
            t = step * UNROLL + u
            r = jnp.where(t < count, tile_row[0, t], ROWBLK)
            col = tile_col[0, t]
            place = place_of(col // COLBLK, depth)
            weights = table[jnp.minimum(r * COLBLK + col % COLBLK, ROWBLK * COLBLK)]
            product = jnp.dot(weights, tiles[0, t], preferred_element_type=F32)
            outgoing[place] = outgoing[place] + product[0:8] + product[8:16]
        return carry

    lax.fori_loop(0, ntile // UNROLL, body, 0)


def final_kernel(
    tiles, tile_row, tile_col, tile_count, gathered, bound_vec, rscale, dual_in, step_in, y_out
):
    scales = rscale[...]
    product = forward_rows(tiles, tile_row, tile_col, tile_count[0], gathered) * scales
    dual = jnp.maximum(
        0.0, dual_in[...] + step_in[...] * (bound_rows(bound_vec) * scales - product)
    )
    for k in range(2):
        for r in range(ROWBLK):
            y_out[k : k + 1, r * 128 : (r + 1) * 128] = dual[k * ROWBLK + r : k * ROWBLK + r + 1]


def primal_rows(ref):
    return jnp.concatenate(
        [ref[k : k + 1, c * 128 : (c + 1) * 128] for c in range(COLBLK) for k in range(2)], axis=0
    )


def exchange(depth, combine, update, outgoing, gathered, scratch):
    (in_plane, reduced, in_line, sem_a, sem_b, sem_c, sem_d) = scratch
    me = lax.axis_index("band")
    z = me // PLANE
    p = me % PLANE
    plane_peers = [(p + d) % PLANE for d in range(1, PLANE)]
    line_peers = [(z + d) % depth for d in range(1, depth)]

    barrier = pltpu.get_barrier_semaphore()
    for q in plane_peers:
        pl.semaphore_signal(
            barrier, inc=1, device_id={"band": z * PLANE + q}, device_id_type=MESH
        )
    for q in line_peers:
        pl.semaphore_signal(
            barrier, inc=1, device_id={"band": q * PLANE + p}, device_id_type=MESH
        )
    pl.semaphore_wait(barrier, len(plane_peers) + len(line_peers))

    def send(src, dst, sems, slot, band):
        copy = pltpu.make_async_remote_copy(
            src_ref=src,
            dst_ref=dst,
            send_sem=sems.at[0, slot],
            recv_sem=sems.at[1, slot],
            device_id={"band": band},
            device_id_type=MESH,
        )
        copy.start()
        return copy

    first = [
        send(
            outgoing.at[pl.ds(q * depth, depth)], in_plane.at[i], sem_a, i, z * PLANE + q
        )
        for i, q in enumerate(plane_peers)
    ]
    total = outgoing[pl.ds(p * depth, depth)]
    for i, copy in enumerate(first):
        copy.wait_recv()
        total = combine(total, in_plane[i])
    reduced[...] = total
    second = [
        send(reduced.at[q], in_line.at[i], sem_b, i, q * PLANE + p)
        for i, q in enumerate(line_peers)
    ]
    mine = reduced[z]
    for i, copy in enumerate(second):
        copy.wait_recv()
        mine = combine(mine, in_line[i])
    block = update(mine)
    at = (p * depth + z) * COLBLK
    for c in range(COLBLK):
        gathered[at + c] = block[2 * c : 2 * c + 2]
    third = [
        send(
            gathered.at[pl.ds(at, COLBLK)], gathered.at[pl.ds(at, COLBLK)], sem_c, i, q * PLANE + p
        )
        for i, q in enumerate(line_peers)
    ]
    for copy in third:
        copy.wait_recv()
    span = depth * COLBLK
    fourth = [
        send(
            gathered.at[pl.ds(p * span, span)],
            gathered.at[pl.ds(p * span, span)],
            sem_d,
            i,
            z * PLANE + q,
        )
        for i, q in enumerate(plane_peers)
    ]
    for copy in fourth:
        copy.wait_recv()
    for copy in first + second + third + fourth:
        copy.wait_send()


def primal_kernel(depth, outgoing, cost, x_start, gathered, primal_out, cscale, primal_step, *scratch):
    def combine(a, b):
        row = lax.broadcasted_iota(jnp.int32, a.shape, a.ndim - 2)
        return jnp.where(row < 4, a + b, jnp.maximum(a, b))

    def update(mine):
        row = lax.broadcasted_iota(jnp.int32, (4, 128), 0)
        scales = lax.rsqrt(
            jnp.where(
                row < 2,
                jnp.broadcast_to(mine[4:5], (4, 128)),
                jnp.broadcast_to(mine[5:6], (4, 128)),
            )
        )
        start = primal_rows(x_start)
        primal = jnp.maximum(
            0.0, start - step_size * (primal_rows(cost) * scales - mine[0:4] * scales)
        )
        primal_out[...] = primal
        cscale[...] = scales
        move = (primal - start) ** 2
        move = move[0:2] + move[2:4]
        zeros = jnp.zeros((4, 128), F32)
        primal_step[...] = jnp.concatenate([zeros, move, zeros[0:2]], axis=0)
        return (2.0 * primal - start) * scales

    exchange(depth, combine, update, outgoing, gathered, scratch)


def second_kernel(depth, outgoing, cost, primal_in, cscale, gathered, x_out, dual_step, *scratch):
    def update(mine):
        row = lax.broadcasted_iota(jnp.int32, (4, 128), 0)
        sums = jnp.sum(mine[4:8], axis=1, keepdims=True) + 1e-06
        omega = jnp.sqrt(sums[2:4] / sums[0:2])
        omega = jnp.broadcast_to(omega, (2, 128))
        wide = jnp.concatenate([omega, omega], axis=0)
        dual_step[...] = jnp.concatenate(
            [
                jnp.broadcast_to(step_size * omega[0:1], (4, 128)),
                jnp.broadcast_to(step_size * omega[1:2], (4, 128)),
            ],
            axis=0,
        )
        scales = cscale[...]
        before = primal_in[...]
        primal = jnp.maximum(
            0.0, before - (step_size / wide) * (primal_rows(cost) * scales - mine[0:4] * scales)
        )
        for c in range(COLBLK):
            x_out[:, c * 128 : (c + 1) * 128] = primal[2 * c : 2 * c + 2]
        return (2.0 * primal - before) * scales

    exchange(depth, lambda a, b: a + b, update, outgoing, gathered, scratch)


VMEM = pl.BlockSpec(memory_space=pltpu.VMEM)
SMEM = pl.BlockSpec(memory_space=pltpu.SMEM)
LIMIT = 40 << 20


def shards(tiles, tile_row, tile_col, tile_count, cost, bound_vec, x_start, y_start):
    bands = lax.axis_size("band")
    depth = bands // PLANE
    bound_vec = bound_vec.reshape(1, -1)

    def shape(*dims):
        return jax.ShapeDtypeStruct(dims, F32)

    index = (tile_row, tile_col, tile_count)
    local = [VMEM, SMEM, SMEM, SMEM]
    params = pltpu.CompilerParams(vmem_limit_bytes=LIMIT)
    table = pltpu.VMEM((ROWBLK * COLBLK + 1, 16, 128), BF16)

    def comm(kernel, ident, out_shape, nin):
        return pl.pallas_call(
            functools.partial(kernel, depth),
            out_shape=out_shape,
            in_specs=[VMEM] * nin,
            out_specs=[VMEM] * len(out_shape),
            scratch_shapes=[
                pltpu.VMEM((PLANE - 1, depth, 8, 128), F32),
                pltpu.VMEM((depth, 8, 128), F32),
                pltpu.VMEM((depth - 1, 8, 128), F32),
                pltpu.SemaphoreType.DMA((2, PLANE - 1)),
                pltpu.SemaphoreType.DMA((2, depth - 1)),
                pltpu.SemaphoreType.DMA((2, depth - 1)),
                pltpu.SemaphoreType.DMA((2, PLANE - 1)),
            ],
            compiler_params=pltpu.CompilerParams(
                collective_id=ident, has_side_effects=True, vmem_limit_bytes=LIMIT
            ),
        )

    outgoing, rscale = pl.pallas_call(
        scale_kernel,
        out_shape=(shape(bands, 8, 128), shape(8, 128)),
        in_specs=local + [VMEM],
        out_specs=(VMEM, VMEM),
        scratch_shapes=[
            pltpu.VMEM((ROWBLK + 1, 128, 128), BF16),
            pltpu.VMEM((ROWBLK + 1, 128, 128), F32),
            table,
        ],
        compiler_params=params,
    )(tiles, *index, y_start)
    gathered, primal, cscale, primal_step = comm(
        primal_kernel,
        0,
        (shape(bands * COLBLK, 2, 128), shape(4, 128), shape(4, 128), shape(8, 128)),
        3,
    )(outgoing, cost, x_start)
    outgoing, dual = pl.pallas_call(
        dual_kernel,
        out_shape=(shape(bands, 8, 128), shape(8, 128)),
        in_specs=local + [VMEM] * 5,
        out_specs=(VMEM, VMEM),
        scratch_shapes=[table],
        compiler_params=params,
    )(tiles, *index, gathered, y_start, bound_vec, rscale, primal_step)
    gathered, x_out, dual_step = comm(
        second_kernel, 1, (shape(bands * COLBLK, 2, 128), shape(2, COLBLK * 128), shape(8, 128)), 4
    )(outgoing, cost, primal, cscale)
    y_out = pl.pallas_call(
        final_kernel,
        out_shape=shape(2, ROWBLK * 128),
        in_specs=local + [VMEM] * 5,
        out_specs=VMEM,
        compiler_params=params,
    )(tiles, *index, gathered, bound_vec, rscale, dual, dual_step)
    return (x_out, y_out)


def solution(mesh):
    return jax.shard_map(
        shards,
        mesh=mesh,
        in_specs=(
            P("band", None, None, None),
            P("band", None),
            P("band", None),
            P("band"),
            P("batch", "band"),
            P("band"),
            P("batch", "band"),
            P("batch", "band"),
        ),
        out_specs=(P("batch", "band"), P("batch", "band")),
        check_vma=False,
    )
```

```python
import jax
import jax.numpy as jnp
from jax import lax
from jax.experimental import pallas as pl
from jax.experimental.pallas import tpu as pltpu
from jax.sharding import PartitionSpec as P

ROWBLK = 4
COLBLK = 2
PLANE = 8
UNROLL = 8
PIECE = 16

step_size = 0.0625
MESH = pl.DeviceIdType.MESH
F32 = jnp.float32
BF16 = jnp.bfloat16


def rows8():
    return lax.broadcasted_iota(jnp.int32, (8, 128), 0)


def split_parts(value):
    high = value.astype(BF16).astype(F32)
    return jnp.concatenate([high, value - high], axis=0).astype(BF16)


def slot_of(offset, depth):
    if isinstance(offset, int):
        return max(2 * offset - 1, 0) if offset <= depth // 2 else 2 * (depth - offset)
    ahead = jnp.maximum(2 * offset - 1, 0)
    return jnp.where(offset <= depth // 2, ahead, 2 * (depth - offset))


def offset_of(slot, depth):
    return (slot + 1) // 2 if slot % 2 == 1 else (depth - slot // 2) % depth


def dual_rows(ref):
    return jnp.concatenate(
        [ref[k : k + 1, r * 128 : (r + 1) * 128] for k in range(2) for r in range(ROWBLK)], axis=0
    )


def bound_rows(ref):
    rows = [ref[0:1, r * 128 : (r + 1) * 128] for r in range(ROWBLK)]
    return jnp.concatenate(rows + rows, axis=0)


def primal_rows(ref):
    return jnp.concatenate(
        [ref[k : k + 1, c * 128 : (c + 1) * 128] for c in range(COLBLK) for k in range(2)], axis=0
    )


def fill_weights(weighted, table):
    row = rows8()
    for r in range(ROWBLK):
        first = jnp.broadcast_to(weighted[r : r + 1], (8, 128))
        second = jnp.broadcast_to(weighted[ROWBLK + r : ROWBLK + r + 1], (8, 128))
        for c in range(COLBLK):
            entry = jnp.where(row == 2 * c, first, jnp.where(row == 2 * c + 1, second, 0.0))
            table[r * COLBLK + c] = split_parts(entry)
    table[ROWBLK * COLBLK] = jnp.zeros((16, 128), BF16)


def kernel(
    tiles_in,
    tile_row,
    tile_col,
    tile_count,
    first_of,
    second_of,
    cost,
    bound_vec,
    x_start,
    y_start,
    x_out,
    y_out,
    tiles,
    flipped,
    spread,
    table,
    parts,
    wide_out,
    wide_in,
    slim_out,
    slim_in,
    steps_out,
    steps_in,
    reduced,
    line_in,
    gathered,
    tile_sem,
    plane_sem,
    steps_sem,
    line_sem,
    back_line_sem,
    back_plane_sem,
):
    ntile = tiles.shape[0]
    depth = reduced.shape[1]
    half = depth // 2
    chunks = ((0, half), (half, depth))
    me = lax.axis_index("band")
    z = me // PLANE
    p = me % PLANE
    plane_peer = {d: z * PLANE + (p + d) % PLANE for d in range(1, PLANE)}
    line_peer = {d: ((z + d) % depth) * PLANE + p for d in range(1, depth)}
    count = tile_count[0]
    row = rows8()
    started = []

    barrier = pltpu.get_barrier_semaphore()
    for band in list(plane_peer.values()) + list(line_peer.values()):
        pl.semaphore_signal(barrier, inc=1, device_id={"band": band}, device_id_type=MESH)

    def piece_copy(i):
        at = pl.ds(i * PIECE, PIECE)
        return pltpu.make_async_copy(tiles_in.at[0, at], tiles.at[at], tile_sem.at[i])

    for i in range(ntile // PIECE):
        piece_copy(i).start()

    def send(src, dst, send_sem, recv_sem, band):
        copy = pltpu.make_async_remote_copy(
            src_ref=src,
            dst_ref=dst,
            send_sem=send_sem,
            recv_sem=recv_sem,
            device_id={"band": band},
            device_id_type=MESH,
        )
        copy.start()
        started.append(copy)
        return copy

    def live_row(t):
        return jnp.where(t < count, tile_row[0, t], ROWBLK)

    def peak_piece(i, peaks):
        piece_copy(i).wait()

        def peak_body(step, peaks):
            peaks = list(peaks)
            for u in range(UNROLL):
                t = i * PIECE + step * UNROLL + u
                r = live_row(t)
                size = jnp.abs(tiles[t])
                for k in range(ROWBLK):
                    peaks[k] = jnp.maximum(peaks[k], jnp.where(r == k, size, jnp.zeros_like(size)))
            return tuple(peaks)

        return lax.fori_loop(0, PIECE // UNROLL, peak_body, peaks)

    peaks = lax.fori_loop(
        0, ntile // PIECE, peak_piece, (jnp.zeros((128, 128), BF16),) * ROWBLK
    )
    lines = []
    for r in range(ROWBLK):
        peak = jnp.max(peaks[r].astype(F32), axis=1, keepdims=True)
        scale = jnp.broadcast_to(lax.rsqrt(peak), (128, 128))
        spread[r] = scale
        lines.append(jnp.transpose(scale)[0:1])
    spread[ROWBLK] = jnp.zeros((128, 128), F32)
    rscale = jnp.concatenate(lines + lines, axis=0)
    start = dual_rows(y_start)
    sbound = bound_rows(bound_vec) * rscale
    fill_weights(start * rscale, table)
    parts[ntile] = jnp.zeros((8, 128), F32)

    def weights_of(t, r):
        return table[jnp.minimum(r * COLBLK + tile_col[0, t] % COLBLK, ROWBLK * COLBLK)]

    def scale_body(step, carry):
        for u in range(UNROLL):
            t = step * UNROLL + u
            r = live_row(t)
            block = tiles[t]
            peak = jnp.max(jnp.abs(block.astype(F32)) * spread[r], axis=0, keepdims=True)
            peak = jnp.broadcast_to(peak, (8, 128))
            product = jnp.dot(weights_of(t, r), block, preferred_element_type=F32)
            parts[t] = jnp.where(
                row < 4,
                product[0:8] + product[8:16],
                jnp.where(row == 4 + tile_col[0, t] % COLBLK, peak, 0.0),
            )
        return carry

    lax.fori_loop(0, ntile // UNROLL, scale_body, 0)

    def adjoint_body(step, carry):
        for u in range(UNROLL):
            t = step * UNROLL + u
            product = jnp.dot(weights_of(t, live_row(t)), tiles[t], preferred_element_type=F32)
            parts[t] = product[0:8] + product[8:16]
        return carry

    def place_parts(store):
        def body(slot, carry):
            odd = slot % 2
            offset = odd * ((slot + 1) // 2) + (1 - odd) * ((depth - slot // 2) % depth)
            for d in range(PLANE):
                owner = ((z + offset) % depth) * PLANE + (p + d) % PLANE
                store(d, slot, parts[first_of[owner]], parts[second_of[owner]])
            return carry

        lax.fori_loop(0, depth, body, 0)

    def store_wide(d, slot, a, b):
        wide_out[d, slot] = jnp.where(row < 4, a + b, jnp.maximum(a, b))

    def store_slim(d, slot, a, b):
        slim_out[d, slot] = (a + b)[0:4]

    def reduce_scatter(turn, out, into, combine, steps=None):
        plane = {}
        if steps is not None:
            steps_out[...] = steps
            for d in range(1, PLANE):
                plane[d] = send(
                    steps_out,
                    steps_in.at[d - 1],
                    steps_sem.at[0, d - 1],
                    steps_sem.at[1, d - 1],
                    plane_peer[d],
                )
        for n, (lo, hi) in reversed(tuple(enumerate(chunks))):
            for d in range(1, PLANE):
                plane[d, n] = send(
                    out.at[d, pl.ds(lo, hi - lo)],
                    into.at[d - 1, pl.ds(lo, hi - lo)],
                    plane_sem.at[turn, 0, n, d - 1],
                    plane_sem.at[turn, 1, n, d - 1],
                    plane_peer[d],
                )
        if steps is not None:
            for d in range(1, PLANE):
                plane[d].wait_recv()
                steps = steps + steps_in[d - 1]
        line = {}
        for n, (lo, hi) in reversed(tuple(enumerate(chunks))):
            total = out[0, lo:hi]
            for d in range(1, PLANE):
                plane[d, n].wait_recv()
                total = combine(total, into[d - 1, lo:hi])
            if steps is None:
                reduced[turn, lo:hi] = total
            else:
                reduced[turn, lo:hi, 0:4] = total
                reduced[turn, lo:hi, 4:8] = jnp.broadcast_to(steps[None], (hi - lo, 4, 128))
            for slot in range(hi - 1, max(lo, 1) - 1, -1):
                back = slot_of((depth - offset_of(slot, depth)) % depth, depth)
                line[back] = send(
                    reduced.at[turn, slot],
                    line_in.at[turn, back],
                    line_sem.at[turn, 0, slot],
                    line_sem.at[turn, 1, back],
                    line_peer[offset_of(slot, depth)],
                )
        return line

    def collect(turn, line, combine):
        mine = reduced[turn, 0]
        for slot in range(1, depth):
            line[slot].wait_recv()
        for slot in range(1, depth):
            mine = combine(mine, line_in[turn, slot])
        return mine

    def all_gather(turn, block):
        for c in range(COLBLK):
            gathered[turn, 0, 0, c] = block[2 * c : 2 * c + 2]
        line = {}
        for slot in range(depth - 1, 0, -1):
            back = slot_of((depth - offset_of(slot, depth)) % depth, depth)
            line[slot] = send(
                gathered.at[turn, 0, 0],
                gathered.at[turn, 0, back],
                back_line_sem.at[turn, 0, slot],
                back_line_sem.at[turn, 1, back],
                line_peer[offset_of(slot, depth)],
            )
        plane = []
        for n, (lo, hi) in enumerate(chunks):
            for slot in range(max(lo, 1), hi):
                pltpu.make_async_remote_copy(
                    src_ref=gathered.at[turn, 0, 0],
                    dst_ref=gathered.at[turn, 0, slot],
                    send_sem=back_line_sem.at[turn, 0, slot],
                    recv_sem=back_line_sem.at[turn, 1, slot],
                    device_id={"band": line_peer[offset_of(slot, depth)]},
                    device_id_type=MESH,
                ).wait_recv()
            for d in range(1, PLANE):
                plane.append(
                    send(
                        gathered.at[turn, 0, pl.ds(lo, hi - lo)],
                        gathered.at[turn, PLANE - d, pl.ds(lo, hi - lo)],
                        back_plane_sem.at[turn, 0, n, d - 1],
                        back_plane_sem.at[turn, 1, n, d - 1],
                        plane_peer[d],
                    )
                )
        for copy in plane:
            copy.wait_recv()

    def forward(turn):
        def body(step, acc):
            for u in range(UNROLL):
                t = step * UNROLL + u
                r = live_row(t)
                col = tile_col[0, t]
                owner = col // COLBLK
                d = (owner % PLANE + PLANE - p) % PLANE
                slot = slot_of((owner // PLANE + depth - z) % depth, depth)
                pair = gathered[turn, d, slot, col % COLBLK]
                value = jnp.where(
                    row < ROWBLK,
                    jnp.broadcast_to(pair[0:1], (8, 128)),
                    jnp.broadcast_to(pair[1:2], (8, 128)),
                )
                value = jnp.where(row % ROWBLK == r, value, 0.0)
                acc = acc + jnp.dot(split_parts(value), flipped[t], preferred_element_type=F32)
            return acc

        acc = lax.fori_loop(0, ntile // UNROLL, body, jnp.zeros((16, 128), F32))
        return (acc[0:8] + acc[8:16]) * rscale

    def join(a, b):
        top = lax.broadcasted_iota(jnp.int32, a.shape, a.ndim - 2) < 4
        return jnp.where(top, a + b, jnp.maximum(a, b))

    def add(a, b):
        return a + b

    place_parts(store_wide)
    pl.semaphore_wait(barrier, PLANE - 1 + depth - 1)
    line = reduce_scatter(0, wide_out, wide_in, join)

    def flip_body(step, carry):
        for u in range(UNROLL):
            t = step * UNROLL + u
            flipped[t] = jnp.transpose(tiles[t])
        return carry

    lax.fori_loop(0, ntile // UNROLL, flip_body, 0)
    mine = collect(0, line, join)

    row4 = lax.broadcasted_iota(jnp.int32, (4, 128), 0)
    cscale = lax.rsqrt(
        jnp.where(
            row4 < 2,
            jnp.broadcast_to(mine[4:5], (4, 128)),
            jnp.broadcast_to(mine[5:6], (4, 128)),
        )
    )
    before = primal_rows(x_start)
    scost = primal_rows(cost) * cscale
    primal = jnp.maximum(0.0, before - step_size * (scost - mine[0:4] * cscale))
    all_gather(0, (2.0 * primal - before) * cscale)
    move = (primal - before) ** 2
    dual = jnp.maximum(0.0, start + step_size * (sbound - forward(0)))
    fill_weights(dual * rscale, table)
    turn = (dual - start) ** 2
    steps = jnp.concatenate(
        [
            move[0:2] + move[2:4],
            jnp.sum(turn[0:4], axis=0, keepdims=True),
            jnp.sum(turn[4:8], axis=0, keepdims=True),
        ],
        axis=0,
    )

    lax.fori_loop(0, ntile // UNROLL, adjoint_body, 0)
    place_parts(store_slim)
    mine = collect(1, reduce_scatter(1, slim_out, slim_in, add, steps), add)
    sums = jnp.sum(mine[4:8], axis=1, keepdims=True) + 1e-06
    omega = jnp.broadcast_to(jnp.sqrt(sums[2:4] / sums[0:2]), (2, 128))
    wide = jnp.concatenate([omega, omega], axis=0)
    after = jnp.maximum(0.0, primal - (step_size / wide) * (scost - mine[0:4] * cscale))
    all_gather(1, (2.0 * after - primal) * cscale)
    for c in range(COLBLK):
        x_out[:, c * 128 : (c + 1) * 128] = after[2 * c : 2 * c + 2]
    pace = jnp.concatenate(
        [
            jnp.broadcast_to(step_size * omega[0:1], (4, 128)),
            jnp.broadcast_to(step_size * omega[1:2], (4, 128)),
        ],
        axis=0,
    )
    last = jnp.maximum(0.0, dual + pace * (sbound - forward(1)))
    for k in range(2):
        for r in range(ROWBLK):
            y_out[k : k + 1, r * 128 : (r + 1) * 128] = last[k * ROWBLK + r : k * ROWBLK + r + 1]
    for copy in started:
        copy.wait_send()


VMEM = pl.BlockSpec(memory_space=pltpu.VMEM)
SMEM = pl.BlockSpec(memory_space=pltpu.SMEM)


def shards(tiles, tile_row, tile_col, tile_count, cost, bound_vec, x_start, y_start):
    ntile = tiles.shape[1]
    bands = lax.axis_size("band")
    depth = bands // PLANE
    index = jnp.arange(ntile, dtype=jnp.int32)[None, :]
    match = (tile_col // COLBLK == jnp.arange(bands, dtype=jnp.int32)[:, None]) & (
        index < tile_count[0]
    )
    first_of = jnp.min(jnp.where(match, index, ntile), axis=1)
    second_of = jnp.max(jnp.where(match, index, -1), axis=1)
    second_of = jnp.where(second_of > first_of, second_of, ntile)

    dma = pltpu.SemaphoreType.DMA
    return pl.pallas_call(
        kernel,
        out_shape=(
            jax.ShapeDtypeStruct((2, COLBLK * 128), F32),
            jax.ShapeDtypeStruct((2, ROWBLK * 128), F32),
        ),
        in_specs=[pl.BlockSpec(memory_space=pl.ANY)] + [SMEM] * 5 + [VMEM] * 4,
        out_specs=(VMEM, VMEM),
        scratch_shapes=[
            pltpu.VMEM((ntile, 128, 128), BF16),
            pltpu.VMEM((ntile, 128, 128), BF16),
            pltpu.VMEM((ROWBLK + 1, 128, 128), F32),
            pltpu.VMEM((ROWBLK * COLBLK + 1, 16, 128), BF16),
            pltpu.VMEM((ntile + 1, 8, 128), F32),
            pltpu.VMEM((PLANE, depth, 8, 128), F32),
            pltpu.VMEM((PLANE - 1, depth, 8, 128), F32),
            pltpu.VMEM((PLANE, depth, 4, 128), F32),
            pltpu.VMEM((PLANE - 1, depth, 4, 128), F32),
            pltpu.VMEM((4, 128), F32),
            pltpu.VMEM((PLANE - 1, 4, 128), F32),
            pltpu.VMEM((2, depth, 8, 128), F32),
            pltpu.VMEM((2, depth, 8, 128), F32),
            pltpu.VMEM((2, PLANE, depth, COLBLK, 2, 128), F32),
            dma((ntile // PIECE,)),
            dma((2, 2, 2, PLANE - 1)),
            dma((2, PLANE - 1)),
            dma((2, 2, depth)),
            dma((2, 2, depth)),
            dma((2, 2, 2, PLANE - 1)),
        ],
        compiler_params=pltpu.CompilerParams(
            collective_id=0, has_side_effects=True, vmem_limit_bytes=48 << 20
        ),
    )(
        tiles,
        tile_row,
        tile_col,
        tile_count,
        first_of,
        second_of,
        cost,
        bound_vec.reshape(1, -1),
        x_start,
        y_start,
    )


def solution(mesh):
    return jax.shard_map(
        shards,
        mesh=mesh,
        in_specs=(
            P("band", None, None, None),
            P("band", None),
            P("band", None),
            P("band"),
            P("batch", "band"),
            P("band"),
            P("batch", "band"),
            P("batch", "band"),
        ),
        out_specs=(P("batch", "band"), P("batch", "band")),
        check_vma=False,
    )
```

```python
import jax
import jax.numpy as jnp
from jax import lax
from jax.experimental import pallas as pl
from jax.experimental.pallas import tpu as pltpu
from jax.sharding import PartitionSpec as P

ROWBLK = 4
COLBLK = 2
CORES = 2
RING = 4
PLANE = CORES * RING
UNROLL = 32
PIECE = 32

step_size = 0.0625
MESH = pl.DeviceIdType.MESH
F32 = jnp.float32
BF16 = jnp.bfloat16


def rows8():
    return lax.broadcasted_iota(jnp.int32, (8, 128), 0)


def split_parts(value):
    high = value.astype(BF16).astype(F32)
    return jnp.concatenate([high, value - high], axis=0).astype(BF16)


def slot_of(offset, depth):
    if isinstance(offset, int):
        return max(2 * offset - 1, 0) if offset <= depth // 2 else 2 * (depth - offset)
    ahead = jnp.maximum(2 * offset - 1, 0)
    return jnp.where(offset <= depth // 2, ahead, 2 * (depth - offset))


def offset_of(slot, depth):
    return (slot + 1) // 2 if slot % 2 == 1 else (depth - slot // 2) % depth


def dual_rows(ref):
    return jnp.concatenate(
        [ref[k : k + 1, r * 128 : (r + 1) * 128] for k in range(2) for r in range(ROWBLK)], axis=0
    )


def bound_rows(ref):
    rows = [ref[0:1, r * 128 : (r + 1) * 128] for r in range(ROWBLK)]
    return jnp.concatenate(rows + rows, axis=0)


def primal_rows(ref):
    return jnp.concatenate(
        [ref[k : k + 1, c * 128 : (c + 1) * 128] for c in range(COLBLK) for k in range(2)], axis=0
    )


def fill_weights(weighted, table):
    row = rows8()
    for r in range(ROWBLK):
        first = jnp.broadcast_to(weighted[r : r + 1], (8, 128))
        second = jnp.broadcast_to(weighted[ROWBLK + r : ROWBLK + r + 1], (8, 128))
        for c in range(COLBLK):
            entry = jnp.where(row == 2 * c, first, jnp.where(row == 2 * c + 1, second, 0.0))
            table[r * COLBLK + c] = split_parts(entry)
    table[ROWBLK * COLBLK] = jnp.zeros((16, 128), BF16)


def fill_index(rows, cols, count, depth, y, z, core, index):
    ntile = rows.shape[1]
    lane = lax.broadcasted_iota(jnp.int32, (8, ntile), 1)
    live = lane < count
    row = jnp.broadcast_to(rows, (8, ntile))
    col = jnp.broadcast_to(cols, (8, ntile))
    part = col & 1
    owner = col >> 1
    side = (owner + core) & 1
    turn = ((owner >> 1) + RING - y) & (RING - 1)
    far = ((owner >> 3) + depth - z) & (depth - 1)
    slot = jnp.where(far <= depth // 2, jnp.maximum(2 * far - 1, 0), 2 * (depth - far))
    place = (side * RING + turn) * depth + slot
    at = lax.broadcasted_iota(jnp.int32, (8, ntile), 0)
    index[0, :, 0:ntile] = jnp.where(
        at == 0,
        jnp.where(live, row, ROWBLK),
        jnp.where(
            at == 1,
            jnp.where(live, row * COLBLK + part, ROWBLK * COLBLK),
            place * COLBLK + part,
        ),
    )
    places = PLANE * depth
    wide = jnp.broadcast_to(jnp.where(live, place, -1)[0:1], (128, ntile)).astype(F32)
    match = jnp.transpose(wide) == lax.broadcasted_iota(jnp.int32, (ntile, 128), 1).astype(F32)
    tile = lax.broadcasted_iota(jnp.int32, (ntile, 128), 0)
    first = jnp.min(jnp.where(match, tile, ntile), axis=0, keepdims=True)
    second = jnp.max(jnp.where(match, tile, -1), axis=0, keepdims=True)
    second = jnp.where(second > first, second, ntile)
    at = lax.broadcasted_iota(jnp.int32, (8, 128), 0)
    index[1] = jnp.where(
        at == 0, jnp.broadcast_to(first, (8, 128)), jnp.broadcast_to(second, (8, 128))
    )


def kernel(
    tiles_in,
    row_in,
    col_in,
    tile_count,
    cost_in,
    bound_in,
    x_in,
    y_in,
    x_out,
    y_out,
    tiles,
    flipped,
    spread,
    table,
    parts,
    wide_out,
    wide_core,
    wide_y,
    slim_out,
    slim_core,
    slim_y,
    steps_out,
    steps_in,
    reduced,
    line_in,
    gathered,
    row_vmem,
    col_vmem,
    cost,
    bound_vec,
    x_start,
    y_start,
    tile_row,
    index_vmem,
    index,
    tile_sem,
    small_sem,
    core_sem,
    ring_sem,
    steps_sem,
    line_sem,
    back_line_sem,
    back_plane_sem,
):
    ntile = tiles.shape[0]
    depth = reduced.shape[1]
    edges = (0, depth // 2, depth - depth // 4, depth) if depth >= 8 else (0, depth // 2, depth)
    chunks = tuple(zip(edges[:-1], edges[1:]))
    nchunk = len(chunks)
    me = lax.axis_index("band")
    z = me // PLANE
    y = (me // CORES) % RING
    core = me % CORES
    plane = [(a, b) for a in range(CORES) for b in range(RING) if (a, b) != (0, 0)]
    plane_peer = {
        (a, b): z * PLANE + ((y + b) % RING) * CORES + (core + a) % CORES for a, b in plane
    }
    line_peer = {d: ((z + d) % depth) * PLANE + me % PLANE for d in range(1, depth)}
    count = tile_count[0]
    row = rows8()
    started = []

    barrier = pltpu.get_barrier_semaphore()
    for band in list(plane_peer.values()) + list(line_peer.values()):
        pl.semaphore_signal(barrier, inc=1, device_id={"band": band}, device_id_type=MESH)

    def piece_copy(i):
        at = pl.ds(i * PIECE, PIECE)
        return pltpu.make_async_copy(tiles_in.at[0, at], tiles.at[at], tile_sem.at[i])

    small = [
        pltpu.make_async_copy(src, dst, small_sem.at[i])
        for i, (src, dst) in enumerate(
            (
                (row_in, tile_row),
                (row_in, row_vmem),
                (col_in, col_vmem),
                (y_in, y_start),
                (bound_in, bound_vec),
                (x_in, x_start),
                (cost_in, cost),
            )
        )
    ]
    index_copy = pltpu.make_async_copy(index_vmem, index, small_sem.at[len(small)])
    for copy in small[:3]:
        copy.start()
    for i in range(ntile // PIECE):
        piece_copy(i).start()
    for copy in small[3:]:
        copy.start()
    small[1].wait()
    small[2].wait()
    fill_index(row_vmem[...], col_vmem[...], count, depth, y, z, core, index_vmem)
    index_copy.start()
    small[0].wait()

    def send(src, dst, send_sem, recv_sem, band):
        copy = pltpu.make_async_remote_copy(
            src_ref=src,
            dst_ref=dst,
            send_sem=send_sem,
            recv_sem=recv_sem,
            device_id={"band": band},
            device_id_type=MESH,
        )
        copy.start()
        started.append(copy)
        return copy

    def live_row(t):
        return jnp.where(t < count, tile_row[0, t], ROWBLK)

    def peak_piece(i, peaks):
        piece_copy(i).wait()

        def peak_body(step, peaks):
            peaks = list(peaks)
            for u in range(UNROLL):
                t = i * PIECE + step * UNROLL + u
                r = live_row(t)
                size = jnp.abs(tiles[t])
                for k in range(ROWBLK):
                    peaks[k] = jnp.maximum(peaks[k], jnp.where(r == k, size, jnp.zeros_like(size)))
            return tuple(peaks)

        return lax.fori_loop(0, PIECE // UNROLL, peak_body, peaks)

    peaks = lax.fori_loop(
        0, ntile // PIECE, peak_piece, (jnp.zeros((128, 128), BF16),) * ROWBLK
    )
    lines = []
    for r in range(ROWBLK):
        peak = jnp.max(peaks[r].astype(F32), axis=1, keepdims=True)
        scale = jnp.broadcast_to(lax.rsqrt(peak), (128, 128))
        spread[r] = scale
        lines.append(jnp.transpose(scale)[0:1])
    spread[ROWBLK] = jnp.zeros((128, 128), F32)
    rscale = jnp.concatenate(lines + lines, axis=0)
    small[3].wait()
    small[4].wait()
    start = dual_rows(y_start)
    sbound = bound_rows(bound_vec) * rscale
    fill_weights(start * rscale, table)
    parts[ntile] = jnp.zeros((8, 128), F32)
    index_copy.wait()

    def scale_body(step, carry):
        for u in range(UNROLL):
            t = step * UNROLL + u
            entry = index[0, 1, t]
            block = tiles[t]
            peak = jnp.max(
                jnp.abs(block.astype(F32)) * spread[index[0, 0, t]], axis=0, keepdims=True
            )
            peak = jnp.broadcast_to(peak, (8, 128))
            product = jnp.dot(table[entry], block, preferred_element_type=F32)
            parts[t] = jnp.where(
                row < 4,
                product[0:8] + product[8:16],
                jnp.where(row == 4 + entry % COLBLK, peak, 0.0),
            )
        return carry

    lax.fori_loop(0, ntile // UNROLL, scale_body, 0)

    def adjoint_body(step, carry):
        for u in range(UNROLL):
            t = step * UNROLL + u
            product = jnp.dot(table[index[0, 1, t]], tiles[t], preferred_element_type=F32)
            parts[t] = product[0:8] + product[8:16]
        return carry

    def place_parts(store):
        def body(slot, carry):
            for a in range(CORES):
                for b in range(RING):
                    at = (a * RING + b) * depth + slot
                    store(a, b, slot, parts[index[1, 0, at]], parts[index[1, 1, at]])
            return carry

        lax.fori_loop(0, depth, body, 0)

    def store_wide(a, b, slot, first, second):
        wide_out[a, b, slot] = jnp.where(row < 4, first + second, jnp.maximum(first, second))

    def store_slim(a, b, slot, first, second):
        slim_out[a, b, slot] = (first + second)[0:4]

    def back_of(slot):
        return slot_of((depth - offset_of(slot, depth)) % depth, depth)

    def reduce_scatter(turn, out, from_core, from_y, combine, steps=None):
        order = tuple(range(nchunk))[::-1]
        sent = {}
        for n in order:
            at = pl.ds(chunks[n][0], chunks[n][1] - chunks[n][0])
            sent[n] = send(
                out.at[1, :, at],
                from_core.at[:, at],
                core_sem.at[turn, 0, n],
                core_sem.at[turn, 1, n],
                plane_peer[1, 0],
            )
        if steps is not None:
            steps_out[...] = steps
            for i, peer in enumerate(plane):
                sent["steps", i] = send(
                    steps_out,
                    steps_in.at[i],
                    steps_sem.at[0, i],
                    steps_sem.at[1, i],
                    plane_peer[peer],
                )
        for n in order:
            lo, hi = chunks[n]
            at = pl.ds(lo, hi - lo)
            sent[n].wait_recv()
            for b in range(RING):
                from_core[b, lo:hi] = combine(out[0, b, lo:hi], from_core[b, lo:hi])
            for b in range(1, RING):
                sent[n, b] = send(
                    from_core.at[b, at],
                    from_y.at[b - 1, at],
                    ring_sem.at[turn, 0, n, b - 1],
                    ring_sem.at[turn, 1, n, b - 1],
                    plane_peer[0, b],
                )
        if steps is not None:
            for i in range(len(plane)):
                sent["steps", i].wait_recv()
                steps = steps + steps_in[i]
        line = {}
        for n in order:
            lo, hi = chunks[n]
            total = from_core[0, lo:hi]
            for b in range(1, RING):
                sent[n, b].wait_recv()
                total = combine(total, from_y[b - 1, lo:hi])
            if steps is None:
                reduced[turn, lo:hi] = total
            else:
                reduced[turn, lo:hi, 0:4] = total
                reduced[turn, lo:hi, 4:8] = jnp.broadcast_to(steps[None], (hi - lo, 4, 128))
            for slot in range(hi - 1, max(lo, 1) - 1, -1):
                back = back_of(slot)
                line[back] = send(
                    reduced.at[turn, slot],
                    line_in.at[turn, back],
                    line_sem.at[turn, 0, slot],
                    line_sem.at[turn, 1, back],
                    line_peer[offset_of(slot, depth)],
                )
        return line

    def collect(turn, line, combine):
        mine = reduced[turn, 0]
        for slot in range(1, depth):
            line[slot].wait_recv()
            mine = combine(mine, line_in[turn, slot])
        return mine

    def all_gather(turn, block):
        for c in range(COLBLK):
            gathered[turn, 0, 0, c] = block[2 * c : 2 * c + 2]
        line = {}
        for slot in range(depth - 1, 0, -1):
            back = back_of(slot)
            line[back] = send(
                gathered.at[turn, 0, 0],
                gathered.at[turn, 0, back],
                back_line_sem.at[turn, 0, slot],
                back_line_sem.at[turn, 1, back],
                line_peer[offset_of(slot, depth)],
            )
        sent = []
        for n, (lo, hi) in enumerate(chunks):
            for slot in range(max(lo, 1), hi):
                line[slot].wait_recv()
            at = pl.ds(lo, hi - lo)
            for i, (a, b) in enumerate(plane):
                sent.append(
                    send(
                        gathered.at[turn, 0, at],
                        gathered.at[turn, a * RING + (RING - b) % RING, at],
                        back_plane_sem.at[turn, 0, n, i],
                        back_plane_sem.at[turn, 1, n, i],
                        plane_peer[a, b],
                    )
                )
        for copy in sent:
            copy.wait_recv()

    def forward(turn):
        def body(step, acc):
            lhs = []
            for u in range(UNROLL):
                t = step * UNROLL + u
                r = index[0, 0, t]
                at = index[0, 2, t]
                pair = gathered[turn, at // (depth * COLBLK), (at // COLBLK) % depth, at % COLBLK]
                value = jnp.where(
                    row < ROWBLK,
                    jnp.broadcast_to(pair[0:1], (8, 128)),
                    jnp.broadcast_to(pair[1:2], (8, 128)),
                )
                lhs.append(split_parts(jnp.where(row % ROWBLK == r, value, 0.0)))
            block = flipped[pl.ds(step * UNROLL, UNROLL)].reshape(UNROLL * 128, 128)
            return acc + jnp.dot(
                jnp.concatenate(lhs, axis=1), block, preferred_element_type=F32
            )

        acc = lax.fori_loop(0, ntile // UNROLL, body, jnp.zeros((16, 128), F32))
        return (acc[0:8] + acc[8:16]) * rscale

    def join(a, b):
        top = lax.broadcasted_iota(jnp.int32, a.shape, a.ndim - 2) < 4
        return jnp.where(top, a + b, jnp.maximum(a, b))

    def add(a, b):
        return a + b

    place_parts(store_wide)
    pl.semaphore_wait(barrier, len(plane_peer) + len(line_peer))
    line = reduce_scatter(0, wide_out, wide_core, wide_y, join)

    def flip_body(step, carry):
        for u in range(UNROLL):
            t = step * UNROLL + u
            flipped[t] = jnp.transpose(tiles[t])
        return carry

    lax.fori_loop(0, ntile // UNROLL, flip_body, 0)
    mine = collect(0, line, join)

    row4 = lax.broadcasted_iota(jnp.int32, (4, 128), 0)
    cscale = lax.rsqrt(
        jnp.where(
            row4 < 2,
            jnp.broadcast_to(mine[4:5], (4, 128)),
            jnp.broadcast_to(mine[5:6], (4, 128)),
        )
    )
    small[5].wait()
    small[6].wait()
    before = primal_rows(x_start)
    scost = primal_rows(cost) * cscale
    primal = jnp.maximum(0.0, before - step_size * (scost - mine[0:4] * cscale))
    all_gather(0, (2.0 * primal - before) * cscale)
    move = (primal - before) ** 2
    dual = jnp.maximum(0.0, start + step_size * (sbound - forward(0)))
    fill_weights(dual * rscale, table)
    turn = (dual - start) ** 2
    steps = jnp.concatenate(
        [
            move[0:2] + move[2:4],
            jnp.sum(turn[0:4], axis=0, keepdims=True),
            jnp.sum(turn[4:8], axis=0, keepdims=True),
        ],
        axis=0,
    )

    lax.fori_loop(0, ntile // UNROLL, adjoint_body, 0)
    place_parts(store_slim)
    mine = collect(1, reduce_scatter(1, slim_out, slim_core, slim_y, add, steps), add)
    sums = jnp.sum(mine[4:8], axis=1, keepdims=True) + 1e-06
    omega = jnp.broadcast_to(jnp.sqrt(sums[2:4] / sums[0:2]), (2, 128))
    wide = jnp.concatenate([omega, omega], axis=0)
    after = jnp.maximum(0.0, primal - (step_size / wide) * (scost - mine[0:4] * cscale))
    all_gather(1, (2.0 * after - primal) * cscale)
    for c in range(COLBLK):
        x_out[:, c * 128 : (c + 1) * 128] = after[2 * c : 2 * c + 2]
    pace = jnp.concatenate(
        [
            jnp.broadcast_to(step_size * omega[0:1], (4, 128)),
            jnp.broadcast_to(step_size * omega[1:2], (4, 128)),
        ],
        axis=0,
    )
    last = jnp.maximum(0.0, dual + pace * (sbound - forward(1)))
    for k in range(2):
        for r in range(ROWBLK):
            y_out[k : k + 1, r * 128 : (r + 1) * 128] = last[k * ROWBLK + r : k * ROWBLK + r + 1]
    for copy in started:
        copy.wait_send()


HBM = pl.BlockSpec(memory_space=pltpu.HBM)
VMEM = pl.BlockSpec(memory_space=pltpu.VMEM)
SMEM = pl.BlockSpec(memory_space=pltpu.SMEM)


def shards(tiles, tile_row, tile_col, tile_count, cost, bound_vec, x_start, y_start):
    ntile = tiles.shape[1]
    depth = lax.axis_size("band") // PLANE
    dma = pltpu.SemaphoreType.DMA
    nchunk = 3 if depth >= 8 else 2
    return pl.pallas_call(
        kernel,
        out_shape=(
            jax.ShapeDtypeStruct((2, COLBLK * 128), F32),
            jax.ShapeDtypeStruct((2, ROWBLK * 128), F32),
        ),
        in_specs=[HBM] * 3 + [SMEM] + [HBM] * 4,
        out_specs=(VMEM, VMEM),
        scratch_shapes=[
            pltpu.VMEM((ntile, 128, 128), BF16),
            pltpu.VMEM((ntile, 128, 128), BF16),
            pltpu.VMEM((ROWBLK + 1, 128, 128), F32),
            pltpu.VMEM((ROWBLK * COLBLK + 1, 16, 128), BF16),
            pltpu.VMEM((ntile + 1, 8, 128), F32),
            pltpu.VMEM((CORES, RING, depth, 8, 128), F32),
            pltpu.VMEM((RING, depth, 8, 128), F32),
            pltpu.VMEM((RING - 1, depth, 8, 128), F32),
            pltpu.VMEM((CORES, RING, depth, 4, 128), F32),
            pltpu.VMEM((RING, depth, 4, 128), F32),
            pltpu.VMEM((RING - 1, depth, 4, 128), F32),
            pltpu.VMEM((4, 128), F32),
            pltpu.VMEM((PLANE - 1, 4, 128), F32),
            pltpu.VMEM((2, depth, 8, 128), F32),
            pltpu.VMEM((2, depth, 8, 128), F32),
            pltpu.VMEM((2, PLANE, depth, COLBLK, 2, 128), F32),
            pltpu.VMEM((1, ntile), jnp.int32),
            pltpu.VMEM((1, ntile), jnp.int32),
            pltpu.VMEM((2, COLBLK * 128), F32),
            pltpu.VMEM((1, ROWBLK * 128), F32),
            pltpu.VMEM((2, COLBLK * 128), F32),
            pltpu.VMEM((2, ROWBLK * 128), F32),
            pltpu.SMEM((1, ntile), jnp.int32),
            pltpu.VMEM((2, 8, 128), jnp.int32),
            pltpu.SMEM((2, 8, 128), jnp.int32),
            dma((ntile // PIECE,)),
            dma((8,)),
            dma((2, 2, nchunk)),
            dma((2, 2, nchunk, RING - 1)),
            dma((2, PLANE - 1)),
            dma((2, 2, depth)),
            dma((2, 2, depth)),
            dma((2, 2, nchunk, PLANE - 1)),
        ],
        compiler_params=pltpu.CompilerParams(
            collective_id=0, has_side_effects=True, vmem_limit_bytes=60 << 20
        ),
    )(
        tiles,
        tile_row,
        tile_col,
        tile_count,
        cost,
        bound_vec.reshape(1, -1),
        x_start,
        y_start,
    )


def solution(mesh):
    return jax.shard_map(
        shards,
        mesh=mesh,
        in_specs=(
            P("band", None, None, None),
            P("band", None),
            P("band", None),
            P("band"),
            P("batch", "band"),
            P("band"),
            P("batch", "band"),
            P("batch", "band"),
        ),
        out_specs=(P("batch", "band"), P("batch", "band")),
        check_vma=False,
    )
```

```python
import jax
import jax.numpy as jnp
from jax import lax
from jax.experimental import pallas as pl
from jax.experimental.pallas import tpu as pltpu
from jax.sharding import PartitionSpec as P

ROWBLK = 4
COLBLK = 2
CORES = 2
RING = 4
PLANE = CORES * RING
UNROLL = 32
PIECE = 32

step_size = 0.0625
MESH = pl.DeviceIdType.MESH
F32 = jnp.float32
BF16 = jnp.bfloat16


def rows8():
    return lax.broadcasted_iota(jnp.int32, (8, 128), 0)


def split_parts(value):
    high = value.astype(BF16).astype(F32)
    return jnp.concatenate([high, value - high], axis=0).astype(BF16)


def slot_of(offset, depth):
    if isinstance(offset, int):
        return max(2 * offset - 1, 0) if offset <= depth // 2 else 2 * (depth - offset)
    ahead = jnp.maximum(2 * offset - 1, 0)
    return jnp.where(offset <= depth // 2, ahead, 2 * (depth - offset))


def offset_of(slot, depth):
    return (slot + 1) // 2 if slot % 2 == 1 else (depth - slot // 2) % depth


def dual_rows(ref):
    return jnp.concatenate(
        [ref[k : k + 1, r * 128 : (r + 1) * 128] for k in range(2) for r in range(ROWBLK)], axis=0
    )


def bound_rows(ref):
    rows = [ref[0:1, r * 128 : (r + 1) * 128] for r in range(ROWBLK)]
    return jnp.concatenate(rows + rows, axis=0)


def primal_rows(ref):
    return jnp.concatenate(
        [ref[k : k + 1, c * 128 : (c + 1) * 128] for c in range(COLBLK) for k in range(2)], axis=0
    )


def fill_weights(weighted, table):
    row = rows8()
    for r in range(ROWBLK):
        first = jnp.broadcast_to(weighted[r : r + 1], (8, 128))
        second = jnp.broadcast_to(weighted[ROWBLK + r : ROWBLK + r + 1], (8, 128))
        for c in range(COLBLK):
            entry = jnp.where(row == 2 * c, first, jnp.where(row == 2 * c + 1, second, 0.0))
            table[r * COLBLK + c] = split_parts(entry)
    table[ROWBLK * COLBLK] = jnp.zeros((16, 128), BF16)


def fill_index(rows, cols, count, depth, y, z, core, index):
    ntile = rows.shape[1]
    lane = lax.broadcasted_iota(jnp.int32, (8, ntile), 1)
    live = lane < count
    row = jnp.broadcast_to(rows, (8, ntile))
    col = jnp.broadcast_to(cols, (8, ntile))
    part = col & 1
    owner = col >> 1
    side = (owner + core) & 1
    turn = ((owner >> 1) + RING - y) & (RING - 1)
    far = ((owner >> 3) + depth - z) & (depth - 1)
    slot = jnp.where(far <= depth // 2, jnp.maximum(2 * far - 1, 0), 2 * (depth - far))
    place = (side * RING + turn) * depth + slot
    at = lax.broadcasted_iota(jnp.int32, (8, ntile), 0)
    index[0, :, 0:ntile] = jnp.where(
        at == 0,
        jnp.where(live, row, ROWBLK),
        jnp.where(
            at == 1,
            jnp.where(live, row * COLBLK + part, ROWBLK * COLBLK),
            place * COLBLK + part,
        ),
    )
    places = PLANE * depth
    wide = jnp.broadcast_to(jnp.where(live, place, -1)[0:1], (128, ntile)).astype(F32)
    match = jnp.transpose(wide) == lax.broadcasted_iota(jnp.int32, (ntile, 128), 1).astype(F32)
    tile = lax.broadcasted_iota(jnp.int32, (ntile, 128), 0)
    first = jnp.min(jnp.where(match, tile, ntile), axis=0, keepdims=True)
    second = jnp.max(jnp.where(match, tile, -1), axis=0, keepdims=True)
    second = jnp.where(second > first, second, ntile)
    at = lax.broadcasted_iota(jnp.int32, (8, 128), 0)
    index[1] = jnp.where(
        at == 0, jnp.broadcast_to(first, (8, 128)), jnp.broadcast_to(second, (8, 128))
    )


def kernel(
    tiles_in,
    row_in,
    col_in,
    tile_count,
    cost_in,
    bound_in,
    x_in,
    y_in,
    x_out,
    y_out,
    tiles,
    flipped,
    spread,
    table,
    parts,
    wide_out,
    wide_core,
    wide_y,
    wide_far,
    slim_out,
    slim_core,
    slim_y,
    slim_far,
    steps_out,
    steps_in,
    reduced,
    line_in,
    gathered,
    row_vmem,
    col_vmem,
    cost,
    bound_vec,
    x_start,
    y_start,
    tile_row,
    index_vmem,
    index,
    tile_sem,
    small_sem,
    core_sem,
    ring_sem,
    far_sem,
    steps_sem,
    line_sem,
    back_line_sem,
    back_plane_sem,
    back_far_sem,
):
    ntile = tiles.shape[0]
    depth = reduced.shape[2]
    edges = (0, depth // 2 - 1, depth - 3) if depth >= 8 else (0, 1)
    chunks = tuple(zip(edges[:-1], edges[1:]))
    nchunk = len(chunks)
    rim = edges[-1]
    far = pl.ds(rim, depth - rim)
    me = lax.axis_index("band")
    z = me // PLANE
    y = (me // CORES) % RING
    core = me % CORES
    plane = [(a, b) for a in range(CORES) for b in range(RING) if (a, b) != (0, 0)]
    plane_peer = {
        (a, b): z * PLANE + ((y + b) % RING) * CORES + (core + a) % CORES for a, b in plane
    }
    line_peer = {d: ((z + d) % depth) * PLANE + me % PLANE for d in range(1, depth)}
    cross_peer = {
        slot: ((z + offset_of(slot, depth)) % depth) * PLANE + me % PLANE + 1 - 2 * core
        for slot in range(rim, depth)
    }
    peers = list(plane_peer.values()) + list(line_peer.values()) + list(cross_peer.values())
    count = tile_count[0]
    row = rows8()
    started = []

    barrier = pltpu.get_barrier_semaphore()
    for band in peers:
        pl.semaphore_signal(barrier, inc=1, device_id={"band": band}, device_id_type=MESH)

    def piece_copy(i):
        at = pl.ds(i * PIECE, PIECE)
        return pltpu.make_async_copy(tiles_in.at[0, at], tiles.at[at], tile_sem.at[i])

    small = [
        pltpu.make_async_copy(src, dst, small_sem.at[i])
        for i, (src, dst) in enumerate(
            (
                (row_in, tile_row),
                (row_in, row_vmem),
                (col_in, col_vmem),
                (y_in, y_start),
                (bound_in, bound_vec),
                (x_in, x_start),
                (cost_in, cost),
            )
        )
    ]
    index_copy = pltpu.make_async_copy(index_vmem, index, small_sem.at[len(small)])
    for copy in small[:3]:
        copy.start()
    for i in range(ntile // PIECE):
        piece_copy(i).start()
    for copy in small[3:]:
        copy.start()
    small[1].wait()
    small[2].wait()
    fill_index(row_vmem[...], col_vmem[...], count, depth, y, z, core, index_vmem)
    index_copy.start()
    small[0].wait()

    def send(src, dst, send_sem, recv_sem, band):
        copy = pltpu.make_async_remote_copy(
            src_ref=src,
            dst_ref=dst,
            send_sem=send_sem,
            recv_sem=recv_sem,
            device_id={"band": band},
            device_id_type=MESH,
        )
        copy.start()
        started.append(copy)
        return copy

    def live_row(t):
        return jnp.where(t < count, tile_row[0, t], ROWBLK)

    def peak_piece(i, peaks):
        piece_copy(i).wait()

        def peak_body(step, peaks):
            peaks = list(peaks)
            for u in range(UNROLL):
                t = i * PIECE + step * UNROLL + u
                r = live_row(t)
                size = jnp.abs(tiles[t])
                for k in range(ROWBLK):
                    peaks[k] = jnp.maximum(peaks[k], jnp.where(r == k, size, jnp.zeros_like(size)))
            return tuple(peaks)

        return lax.fori_loop(0, PIECE // UNROLL, peak_body, peaks)

    peaks = lax.fori_loop(
        0, ntile // PIECE, peak_piece, (jnp.zeros((128, 128), BF16),) * ROWBLK
    )
    lines = []
    for r in range(ROWBLK):
        peak = jnp.max(peaks[r].astype(F32), axis=1, keepdims=True)
        scale = jnp.broadcast_to(lax.rsqrt(peak), (128, 128))
        spread[r] = scale
        lines.append(jnp.transpose(scale)[0:1])
    spread[ROWBLK] = jnp.zeros((128, 128), F32)
    rscale = jnp.concatenate(lines + lines, axis=0)
    small[3].wait()
    small[4].wait()
    start = dual_rows(y_start)
    sbound = bound_rows(bound_vec) * rscale
    fill_weights(start * rscale, table)
    parts[ntile] = jnp.zeros((8, 128), F32)
    index_copy.wait()

    def scale_body(step, carry):
        for u in range(UNROLL):
            t = step * UNROLL + u
            entry = index[0, 1, t]
            block = tiles[t]
            peak = jnp.max(
                jnp.abs(block.astype(F32)) * spread[index[0, 0, t]], axis=0, keepdims=True
            )
            peak = jnp.broadcast_to(peak, (8, 128))
            product = jnp.dot(table[entry], block, preferred_element_type=F32)
            parts[t] = jnp.where(
                row < 4,
                product[0:8] + product[8:16],
                jnp.where(row == 4 + (entry & 1), peak, 0.0),
            )
        return carry

    lax.fori_loop(0, ntile // UNROLL, scale_body, 0)

    def adjoint_body(step, carry):
        for u in range(UNROLL):
            t = step * UNROLL + u
            product = jnp.dot(table[index[0, 1, t]], tiles[t], preferred_element_type=F32)
            parts[t] = product[0:8] + product[8:16]
        return carry

    def place_parts(store):
        def body(slot, carry):
            for a in range(CORES):
                for b in range(RING):
                    at = (a * RING + b) * depth + slot
                    store(a, b, slot, parts[index[1, 0, at]], parts[index[1, 1, at]])
            return carry

        lax.fori_loop(0, depth, body, 0)

    def store_wide(a, b, slot, first, second):
        wide_out[a, b, slot] = jnp.where(row < 4, first + second, jnp.maximum(first, second))

    def store_slim(a, b, slot, first, second):
        slim_out[a, b, slot] = (first + second)[0:4]

    def back_of(slot):
        return slot_of((depth - offset_of(slot, depth)) % depth, depth)

    def reduce_scatter(turn, out, from_core, from_y, from_far, combine, steps=None):
        order = tuple(range(nchunk))[::-1]
        sent = {}
        for b in range(1, RING):
            sent["far", b] = send(
                out.at[:, b, far],
                from_far.at[b - 1],
                far_sem.at[turn, 0, b - 1],
                far_sem.at[turn, 1, b - 1],
                plane_peer[0, b],
            )
        for n in order:
            at = pl.ds(chunks[n][0], chunks[n][1] - chunks[n][0])
            sent[n] = send(
                out.at[1, :, at],
                from_core.at[:, at],
                core_sem.at[turn, 0, n],
                core_sem.at[turn, 1, n],
                plane_peer[1, 0],
            )
        if steps is not None:
            steps_out[...] = steps
            for i, peer in enumerate(plane):
                sent["steps", i] = send(
                    steps_out,
                    steps_in.at[i],
                    steps_sem.at[0, i],
                    steps_sem.at[1, i],
                    plane_peer[peer],
                )
        for n in order:
            lo, hi = chunks[n]
            at = pl.ds(lo, hi - lo)
            sent[n].wait_recv()
            for b in range(RING):
                from_core[b, lo:hi] = combine(out[0, b, lo:hi], from_core[b, lo:hi])
            for b in range(1, RING):
                sent[n, b] = send(
                    from_core.at[b, at],
                    from_y.at[b - 1, at],
                    ring_sem.at[turn, 0, n, b - 1],
                    ring_sem.at[turn, 1, n, b - 1],
                    plane_peer[0, b],
                )

        def keep(a, lo, hi, total):
            if steps is None:
                reduced[turn, a, lo:hi] = total
            else:
                reduced[turn, a, lo:hi, 0:4] = total
                extra = steps if a == 0 else jnp.zeros_like(steps)
                reduced[turn, a, lo:hi, 4:8] = jnp.broadcast_to(extra[None], (hi - lo, 4, 128))

        if steps is not None:
            for i in range(len(plane)):
                sent["steps", i].wait_recv()
                steps = steps + steps_in[i]
        for b in range(1, RING):
            sent["far", b].wait_recv()
        for a in range(CORES):
            total = out[a, 0, rim:depth]
            for b in range(1, RING):
                total = combine(total, from_far[b - 1, a])
            keep(a, rim, depth, total)
        line = {}

        def along(a, slot):
            back = back_of(slot)
            line[a, back] = send(
                reduced.at[turn, a, slot],
                line_in.at[turn, a, back],
                line_sem.at[turn, a, 0, slot],
                line_sem.at[turn, a, 1, back],
                cross_peer[slot] if a else line_peer[offset_of(slot, depth)],
            )

        for slot in range(depth - 1, rim - 1, -1):
            for a in range(CORES):
                along(a, slot)
        for n in order:
            lo, hi = chunks[n]
            total = from_core[0, lo:hi]
            for b in range(1, RING):
                sent[n, b].wait_recv()
                total = combine(total, from_y[b - 1, lo:hi])
            keep(0, lo, hi, total)
            for slot in range(hi - 1, max(lo, 1) - 1, -1):
                along(0, slot)
        return line

    def collect(turn, line, combine):
        mine = reduced[turn, 0, 0]
        for slot in range(1, depth):
            for a in range(CORES if slot >= rim else 1):
                line[a, slot].wait_recv()
                mine = combine(mine, line_in[turn, a, slot])
        return mine

    def all_gather(turn, block):
        for c in range(COLBLK):
            gathered[turn, 0, 0, c] = block[2 * c : 2 * c + 2]
        line = {}
        for slot in range(depth - 1, 0, -1):
            back = back_of(slot)
            for a in range(CORES if slot >= rim else 1):
                line[a, back] = send(
                    gathered.at[turn, 0, 0, pl.ds(0, COLBLK)],
                    gathered.at[turn, a, 0, pl.ds(back * COLBLK, COLBLK)],
                    back_line_sem.at[turn, a, 0, slot],
                    back_line_sem.at[turn, a, 1, back],
                    cross_peer[slot] if a else line_peer[offset_of(slot, depth)],
                )
        sent = []
        for n, (lo, hi) in enumerate(chunks):
            for slot in range(max(lo, 1), hi):
                line[0, slot].wait_recv()
            at = pl.ds(lo * COLBLK, (hi - lo) * COLBLK)
            for i, (a, b) in enumerate(plane):
                sent.append(
                    send(
                        gathered.at[turn, 0, 0, at],
                        gathered.at[turn, a, (RING - b) % RING, at],
                        back_plane_sem.at[turn, 0, n, i],
                        back_plane_sem.at[turn, 1, n, i],
                        plane_peer[a, b],
                    )
                )
        edge = pl.ds(rim * COLBLK, (depth - rim) * COLBLK)
        for slot in range(rim, depth):
            for a in range(CORES):
                line[a, slot].wait_recv()
        for b in range(1, RING):
            sent.append(
                send(
                    gathered.at[turn, :, 0, edge],
                    gathered.at[turn, :, RING - b, edge],
                    back_far_sem.at[turn, 0, b - 1],
                    back_far_sem.at[turn, 1, b - 1],
                    plane_peer[0, b],
                )
            )
        for copy in sent:
            copy.wait_recv()

    bits = (depth * COLBLK).bit_length() - 1

    def forward(turn):
        def body(step, acc):
            lhs = []
            for u in range(UNROLL):
                t = step * UNROLL + u
                r = index[0, 0, t]
                at = index[0, 2, t]
                side = at >> (bits + 2)
                pair = gathered[turn, side, (at >> bits) & (RING - 1), at & (depth * COLBLK - 1)]
                value = jnp.where(
                    row < ROWBLK,
                    jnp.broadcast_to(pair[0:1], (8, 128)),
                    jnp.broadcast_to(pair[1:2], (8, 128)),
                )
                lhs.append(split_parts(jnp.where(row % ROWBLK == r, value, 0.0)))
            block = flipped[pl.ds(step * UNROLL, UNROLL)].reshape(UNROLL * 128, 128)
            return acc + jnp.dot(
                jnp.concatenate(lhs, axis=1), block, preferred_element_type=F32
            )

        acc = lax.fori_loop(0, ntile // UNROLL, body, jnp.zeros((16, 128), F32))
        return (acc[0:8] + acc[8:16]) * rscale

    def join(a, b):
        top = lax.broadcasted_iota(jnp.int32, a.shape, a.ndim - 2) < 4
        return jnp.where(top, a + b, jnp.maximum(a, b))

    def add(a, b):
        return a + b

    place_parts(store_wide)
    pl.semaphore_wait(barrier, len(peers))
    line = reduce_scatter(0, wide_out, wide_core, wide_y, wide_far, join)

    def flip_body(step, carry):
        for u in range(UNROLL):
            t = step * UNROLL + u
            flipped[t] = jnp.transpose(tiles[t])
        return carry

    lax.fori_loop(0, ntile // UNROLL, flip_body, 0)
    mine = collect(0, line, join)

    row4 = lax.broadcasted_iota(jnp.int32, (4, 128), 0)
    cscale = lax.rsqrt(
        jnp.where(
            row4 < 2,
            jnp.broadcast_to(mine[4:5], (4, 128)),
            jnp.broadcast_to(mine[5:6], (4, 128)),
        )
    )
    small[5].wait()
    small[6].wait()
    before = primal_rows(x_start)
    scost = primal_rows(cost) * cscale
    primal = jnp.maximum(0.0, before - step_size * (scost - mine[0:4] * cscale))
    all_gather(0, (2.0 * primal - before) * cscale)
    move = (primal - before) ** 2
    dual = jnp.maximum(0.0, start + step_size * (sbound - forward(0)))
    fill_weights(dual * rscale, table)
    turn = (dual - start) ** 2
    steps = jnp.concatenate(
        [
            move[0:2] + move[2:4],
            jnp.sum(turn[0:4], axis=0, keepdims=True),
            jnp.sum(turn[4:8], axis=0, keepdims=True),
        ],
        axis=0,
    )

    lax.fori_loop(0, ntile // UNROLL, adjoint_body, 0)
    place_parts(store_slim)
    line = reduce_scatter(
        1, slim_out, slim_core, slim_y, slim_far, add, steps
    )
    mine = collect(1, line, add)
    sums = jnp.sum(mine[4:8], axis=1, keepdims=True) + 1e-06
    omega = jnp.broadcast_to(jnp.sqrt(sums[2:4] / sums[0:2]), (2, 128))
    wide = jnp.concatenate([omega, omega], axis=0)
    after = jnp.maximum(0.0, primal - (step_size / wide) * (scost - mine[0:4] * cscale))
    all_gather(1, (2.0 * after - primal) * cscale)
    for c in range(COLBLK):
        x_out[:, c * 128 : (c + 1) * 128] = after[2 * c : 2 * c + 2]
    pace = jnp.concatenate(
        [
            jnp.broadcast_to(step_size * omega[0:1], (4, 128)),
            jnp.broadcast_to(step_size * omega[1:2], (4, 128)),
        ],
        axis=0,
    )
    last = jnp.maximum(0.0, dual + pace * (sbound - forward(1)))
    for k in range(2):
        for r in range(ROWBLK):
            y_out[k : k + 1, r * 128 : (r + 1) * 128] = last[k * ROWBLK + r : k * ROWBLK + r + 1]
    for copy in started:
        copy.wait_send()


HBM = pl.BlockSpec(memory_space=pltpu.HBM)
VMEM = pl.BlockSpec(memory_space=pltpu.VMEM)
SMEM = pl.BlockSpec(memory_space=pltpu.SMEM)


def shards(tiles, tile_row, tile_col, tile_count, cost, bound_vec, x_start, y_start):
    ntile = tiles.shape[1]
    depth = lax.axis_size("band") // PLANE
    dma = pltpu.SemaphoreType.DMA
    nchunk, rim = (2, depth - 3) if depth >= 8 else (1, 1)
    return pl.pallas_call(
        kernel,
        out_shape=(
            jax.ShapeDtypeStruct((2, COLBLK * 128), F32),
            jax.ShapeDtypeStruct((2, ROWBLK * 128), F32),
        ),
        in_specs=[HBM] * 3 + [SMEM] + [HBM] * 4,
        out_specs=(VMEM, VMEM),
        scratch_shapes=[
            pltpu.VMEM((ntile, 128, 128), BF16),
            pltpu.VMEM((ntile, 128, 128), BF16),
            pltpu.VMEM((ROWBLK + 1, 128, 128), F32),
            pltpu.VMEM((ROWBLK * COLBLK + 1, 16, 128), BF16),
            pltpu.VMEM((ntile + 1, 8, 128), F32),
            pltpu.VMEM((CORES, RING, depth, 8, 128), F32),
            pltpu.VMEM((RING, depth, 8, 128), F32),
            pltpu.VMEM((RING - 1, depth, 8, 128), F32),
            pltpu.VMEM((RING - 1, CORES, depth - rim, 8, 128), F32),
            pltpu.VMEM((CORES, RING, depth, 4, 128), F32),
            pltpu.VMEM((RING, depth, 4, 128), F32),
            pltpu.VMEM((RING - 1, depth, 4, 128), F32),
            pltpu.VMEM((RING - 1, CORES, depth - rim, 4, 128), F32),
            pltpu.VMEM((4, 128), F32),
            pltpu.VMEM((PLANE - 1, 4, 128), F32),
            pltpu.VMEM((2, CORES, depth, 8, 128), F32),
            pltpu.VMEM((2, CORES, depth, 8, 128), F32),
            pltpu.VMEM((2, CORES, RING, depth * COLBLK, 2, 128), F32),
            pltpu.VMEM((1, ntile), jnp.int32),
            pltpu.VMEM((1, ntile), jnp.int32),
            pltpu.VMEM((2, COLBLK * 128), F32),
            pltpu.VMEM((1, ROWBLK * 128), F32),
            pltpu.VMEM((2, COLBLK * 128), F32),
            pltpu.VMEM((2, ROWBLK * 128), F32),
            pltpu.SMEM((1, ntile), jnp.int32),
            pltpu.VMEM((2, 8, 128), jnp.int32),
            pltpu.SMEM((2, 8, 128), jnp.int32),
            dma((ntile // PIECE,)),
            dma((8,)),
            dma((2, 2, nchunk)),
            dma((2, 2, nchunk, RING - 1)),
            dma((2, 2, RING - 1)),
            dma((2, PLANE - 1)),
            dma((2, CORES, 2, depth)),
            dma((2, CORES, 2, depth)),
            dma((2, 2, nchunk, PLANE - 1)),
            dma((2, 2, RING - 1)),
        ],
        compiler_params=pltpu.CompilerParams(
            collective_id=0, has_side_effects=True, vmem_limit_bytes=60 << 20
        ),
    )(
        tiles,
        tile_row,
        tile_col,
        tile_count,
        cost,
        bound_vec.reshape(1, -1),
        x_start,
        y_start,
    )


def solution(mesh):
    return jax.shard_map(
        shards,
        mesh=mesh,
        in_specs=(
            P("band", None, None, None),
            P("band", None),
            P("band", None),
            P("band"),
            P("batch", "band"),
            P("band"),
            P("batch", "band"),
            P("batch", "band"),
        ),
        out_specs=(P("batch", "band"), P("batch", "band")),
        check_vma=False,
    )
```

```python
import jax
import jax.numpy as jnp
from jax import lax
from jax.experimental import pallas as pl
from jax.experimental.pallas import tpu as pltpu
from jax.sharding import PartitionSpec as P

ROWBLK = 4
COLBLK = 2
CORES = 2
RING = 4
PLANE = CORES * RING
UNROLL = 64
PIECE = 64

step_size = 0.0625
MESH = pl.DeviceIdType.MESH
F32 = jnp.float32
BF16 = jnp.bfloat16


def rows8():
    return lax.broadcasted_iota(jnp.int32, (8, 128), 0)


def split_parts(value):
    high = value.astype(BF16).astype(F32)
    return jnp.concatenate([high, value - high], axis=0).astype(BF16)


def slot_of(offset, depth):
    if isinstance(offset, int):
        return max(2 * offset - 1, 0) if offset <= depth // 2 else 2 * (depth - offset)
    ahead = jnp.maximum(2 * offset - 1, 0)
    return jnp.where(offset <= depth // 2, ahead, 2 * (depth - offset))


def offset_of(slot, depth):
    return (slot + 1) // 2 if slot % 2 == 1 else (depth - slot // 2) % depth


def dual_rows(ref):
    return jnp.concatenate(
        [ref[k : k + 1, r * 128 : (r + 1) * 128] for k in range(2) for r in range(ROWBLK)], axis=0
    )


def bound_rows(ref):
    rows = [ref[0:1, r * 128 : (r + 1) * 128] for r in range(ROWBLK)]
    return jnp.concatenate(rows + rows, axis=0)


def primal_rows(ref):
    return jnp.concatenate(
        [ref[k : k + 1, c * 128 : (c + 1) * 128] for c in range(COLBLK) for k in range(2)], axis=0
    )


def fill_weights(weighted, table):
    row = rows8()
    for r in range(ROWBLK):
        first = jnp.broadcast_to(weighted[r : r + 1], (8, 128))
        second = jnp.broadcast_to(weighted[ROWBLK + r : ROWBLK + r + 1], (8, 128))
        for c in range(COLBLK):
            entry = jnp.where(row == 2 * c, first, jnp.where(row == 2 * c + 1, second, 0.0))
            table[r * COLBLK + c] = split_parts(entry)
    table[ROWBLK * COLBLK] = jnp.zeros((16, 128), BF16)


def fill_index(rows, cols, count, depth, y, z, core, index):
    ntile = rows.shape[1]
    lane = lax.broadcasted_iota(jnp.int32, (8, ntile), 1)
    live = lane < count
    row = jnp.broadcast_to(rows, (8, ntile))
    col = jnp.broadcast_to(cols, (8, ntile))
    part = col & 1
    owner = col >> 1
    side = (owner + core) & 1
    turn = ((owner >> 1) + RING - y) & (RING - 1)
    far = ((owner >> 3) + depth - z) & (depth - 1)
    slot = jnp.where(far <= depth // 2, jnp.maximum(2 * far - 1, 0), 2 * (depth - far))
    place = (side * RING + turn) * depth + slot
    at = lax.broadcasted_iota(jnp.int32, (8, ntile), 0)
    index[0, :, 0:ntile] = jnp.where(
        at == 0,
        jnp.where(live, row, ROWBLK),
        jnp.where(
            at == 1,
            jnp.where(live, row * COLBLK + part, ROWBLK * COLBLK),
            place * COLBLK + part,
        ),
    )
    places = PLANE * depth
    wide = jnp.broadcast_to(jnp.where(live, place, -1)[0:1], (128, ntile)).astype(F32)
    match = jnp.transpose(wide) == lax.broadcasted_iota(jnp.int32, (ntile, 128), 1).astype(F32)
    tile = lax.broadcasted_iota(jnp.int32, (ntile, 128), 0)
    first = jnp.min(jnp.where(match, tile, ntile), axis=0, keepdims=True)
    second = jnp.max(jnp.where(match, tile, -1), axis=0, keepdims=True)
    second = jnp.where(second > first, second, ntile)
    at = lax.broadcasted_iota(jnp.int32, (8, 128), 0)
    index[1] = jnp.where(
        at == 0, jnp.broadcast_to(first, (8, 128)), jnp.broadcast_to(second, (8, 128))
    )


def kernel(
    tiles_in,
    row_in,
    col_in,
    tile_count,
    cost_in,
    bound_in,
    x_in,
    y_in,
    x_out,
    y_out,
    tiles,
    flipped,
    spread,
    table,
    parts,
    wide_out,
    wide_core,
    wide_y,
    wide_far,
    slim_out,
    slim_core,
    slim_y,
    slim_far,
    steps_out,
    steps_in,
    reduced,
    line_in,
    gathered,
    row_vmem,
    col_vmem,
    cost,
    bound_vec,
    x_start,
    y_start,
    tile_row,
    index_vmem,
    index,
    tile_sem,
    small_sem,
    core_sem,
    ring_sem,
    far_sem,
    steps_sem,
    line_sem,
    back_line_sem,
    back_plane_sem,
    back_far_sem,
):
    ntile = tiles.shape[0]
    depth = reduced.shape[2]
    edges = (0, depth // 2 - 1, depth - 3) if depth >= 8 else (0, 1)
    chunks = tuple(zip(edges[:-1], edges[1:]))
    nchunk = len(chunks)
    rim = edges[-1]
    far = pl.ds(rim, depth - rim)
    me = lax.axis_index("band")
    z = me // PLANE
    y = (me // CORES) % RING
    core = me % CORES
    plane = [(a, b) for a in range(CORES) for b in range(RING) if (a, b) != (0, 0)]
    plane_peer = {
        (a, b): z * PLANE + ((y + b) % RING) * CORES + (core + a) % CORES for a, b in plane
    }
    line_peer = {d: ((z + d) % depth) * PLANE + me % PLANE for d in range(1, depth)}
    cross_peer = {
        slot: ((z + offset_of(slot, depth)) % depth) * PLANE + me % PLANE + 1 - 2 * core
        for slot in range(rim, depth)
    }
    peers = list(plane_peer.values()) + list(line_peer.values()) + list(cross_peer.values())
    count = tile_count[0]
    row = rows8()
    started = []

    barrier = pltpu.get_barrier_semaphore()
    for band in peers:
        pl.semaphore_signal(barrier, inc=1, device_id={"band": band}, device_id_type=MESH)

    def piece_copy(i):
        at = pl.ds(i * PIECE, PIECE)
        return pltpu.make_async_copy(tiles_in.at[0, at], tiles.at[at], tile_sem.at[i])

    small = [
        pltpu.make_async_copy(src, dst, small_sem.at[i])
        for i, (src, dst) in enumerate(
            (
                (row_in, tile_row),
                (row_in, row_vmem),
                (col_in, col_vmem),
                (y_in, y_start),
                (bound_in, bound_vec),
                (x_in, x_start),
                (cost_in, cost),
            )
        )
    ]
    index_copy = pltpu.make_async_copy(index_vmem, index, small_sem.at[len(small)])
    for copy in small[:3]:
        copy.start()
    for i in range(ntile // PIECE):
        piece_copy(i).start()
    for copy in small[3:]:
        copy.start()
    small[1].wait()
    small[2].wait()
    fill_index(row_vmem[...], col_vmem[...], count, depth, y, z, core, index_vmem)
    index_copy.start()
    small[0].wait()

    def send(src, dst, send_sem, recv_sem, band):
        copy = pltpu.make_async_remote_copy(
            src_ref=src,
            dst_ref=dst,
            send_sem=send_sem,
            recv_sem=recv_sem,
            device_id={"band": band},
            device_id_type=MESH,
        )
        copy.start()
        started.append(copy)
        return copy

    def drain(kept=0):
        done = started[: len(started) - kept]
        del started[: len(done)]
        for copy in done:
            copy.wait_send()

    def live_row(t):
        return jnp.where(t < count, tile_row[0, t], ROWBLK)

    def peak_piece(i, peaks):
        piece_copy(i).wait()

        def peak_body(step, peaks):
            peaks = list(peaks)
            for u in range(UNROLL):
                t = i * PIECE + step * UNROLL + u
                r = live_row(t)
                size = jnp.abs(tiles[t])
                for k in range(ROWBLK):
                    peaks[k] = jnp.maximum(peaks[k], jnp.where(r == k, size, jnp.zeros_like(size)))
            return tuple(peaks)

        return lax.fori_loop(0, PIECE // UNROLL, peak_body, peaks)

    peaks = lax.fori_loop(
        0, ntile // PIECE, peak_piece, (jnp.zeros((128, 128), BF16),) * ROWBLK
    )
    lines = []
    for r in range(ROWBLK):
        peak = jnp.max(peaks[r].astype(F32), axis=1, keepdims=True)
        scale = jnp.broadcast_to(lax.rsqrt(peak), (128, 128))
        spread[r] = scale
        lines.append(jnp.transpose(scale)[0:1])
    spread[ROWBLK] = jnp.zeros((128, 128), F32)
    rscale = jnp.concatenate(lines + lines, axis=0)
    small[3].wait()
    small[4].wait()
    start = dual_rows(y_start)
    sbound = bound_rows(bound_vec) * rscale
    fill_weights(start * rscale, table)
    parts[ntile] = jnp.zeros((8, 128), F32)
    index_copy.wait()

    def scale_body(step, carry):
        for u in range(UNROLL):
            t = step * UNROLL + u
            entry = index[0, 1, t]
            block = tiles[t]
            peak = jnp.max(
                jnp.abs(block.astype(F32)) * spread[index[0, 0, t]], axis=0, keepdims=True
            )
            peak = jnp.broadcast_to(peak, (8, 128))
            product = jnp.dot(table[entry], block, preferred_element_type=F32)
            parts[t] = jnp.where(
                row < 4,
                product[0:8] + product[8:16],
                jnp.where(row == 4 + (entry & 1), peak, 0.0),
            )
        return carry

    lax.fori_loop(0, ntile // UNROLL, scale_body, 0)

    def adjoint_body(step, carry):
        for u in range(UNROLL):
            t = step * UNROLL + u
            product = jnp.dot(table[index[0, 1, t]], tiles[t], preferred_element_type=F32)
            parts[t] = product[0:8] + product[8:16]
        return carry

    def place_parts(store, lo, hi):
        def body(slot, carry):
            for a in range(CORES):
                for b in range(RING):
                    at = (a * RING + b) * depth + slot
                    store(a, b, slot, parts[index[1, 0, at]], parts[index[1, 1, at]])
            return carry

        lax.fori_loop(lo, hi, body, 0)

    def store_wide(a, b, slot, first, second):
        wide_out[a, b, slot] = jnp.where(row < 4, first + second, jnp.maximum(first, second))

    def store_slim(a, b, slot, first, second):
        slim_out[a, b, slot] = (first + second)[0:4]

    def back_of(slot):
        return slot_of((depth - offset_of(slot, depth)) % depth, depth)

    def reduce_scatter(turn, store, out, from_core, from_y, from_far, combine, steps=None):
        order = tuple(range(nchunk))[::-1]
        sent = {}

        def send_steps(kind, b):
            sent["steps", kind, b] = send(
                steps_out.at[kind],
                steps_in.at[kind, b],
                steps_sem.at[0, kind, b],
                steps_sem.at[1, kind, b],
                plane_peer[0, b] if b else plane_peer[1, 0],
            )

        place_parts(store, rim, depth)
        if steps is not None:
            steps_out[0] = steps
            for b in range(RING):
                send_steps(0, b)
        else:
            pl.semaphore_wait(barrier, len(peers))
        for b in range(1, RING):
            sent["far", b] = send(
                out.at[:, b, far],
                from_far.at[b - 1],
                far_sem.at[turn, 0, b - 1],
                far_sem.at[turn, 1, b - 1],
                plane_peer[0, b],
            )
        for n in order:
            at = pl.ds(chunks[n][0], chunks[n][1] - chunks[n][0])
            place_parts(store, *chunks[n])
            sent[n] = send(
                out.at[1, :, at],
                from_core.at[:, at],
                core_sem.at[turn, 0, n],
                core_sem.at[turn, 1, n],
                plane_peer[1, 0],
            )
        if steps is not None:
            sent["steps", 0, 0].wait_recv()
            both = steps + steps_in[0, 0]
            steps_out[1] = both
            for b in range(1, RING):
                send_steps(1, b)
        for n in order:
            lo, hi = chunks[n]
            at = pl.ds(lo, hi - lo)
            sent[n].wait_recv()
            for b in range(RING):
                from_core[b, lo:hi] = combine(out[0, b, lo:hi], from_core[b, lo:hi])
            for b in range(1, RING):
                sent[n, b] = send(
                    from_core.at[b, at],
                    from_y.at[b - 1, at],
                    ring_sem.at[turn, 0, n, b - 1],
                    ring_sem.at[turn, 1, n, b - 1],
                    plane_peer[0, b],
                )

        def keep(a, lo, hi, total, extra):
            if extra is None:
                reduced[turn, a, lo:hi] = total
            else:
                reduced[turn, a, lo:hi, 0:4] = total
                reduced[turn, a, lo:hi, 4:8] = jnp.broadcast_to(extra[None], (hi - lo, 4, 128))

        if steps is not None:
            for b in range(1, RING):
                sent["steps", 0, b].wait_recv()
                steps = steps + steps_in[0, b]
        for b in range(1, RING):
            sent["far", b].wait_recv()
        for a in range(CORES):
            total = out[a, 0, rim:depth]
            for b in range(1, RING):
                total = combine(total, from_far[b - 1, a])
            keep(a, rim, depth, total, steps)
        line = {}

        def along(a, slot):
            back = back_of(slot)
            line[a, back] = send(
                reduced.at[turn, a, slot],
                line_in.at[turn, a, back],
                line_sem.at[turn, a, 0, slot],
                line_sem.at[turn, a, 1, back],
                cross_peer[slot] if a else line_peer[offset_of(slot, depth)],
            )

        for slot in range(depth - 1, rim - 1, -1):
            for a in range(CORES):
                along(a, slot)
        if steps is not None:
            for b in range(1, RING):
                sent["steps", 1, b].wait_recv()
                both = both + steps_in[1, b]
            steps = both
        for n in order:
            lo, hi = chunks[n]
            total = from_core[0, lo:hi]
            for b in range(1, RING):
                sent[n, b].wait_recv()
                total = combine(total, from_y[b - 1, lo:hi])
            keep(0, lo, hi, total, steps)
            for slot in range(hi - 1, max(lo, 1) - 1, -1):
                along(0, slot)
        return line

    def collect(turn, line, combine):
        mine = reduced[turn, 0, 0]
        for slot in range(1, depth):
            for a in range(CORES if slot >= rim else 1):
                line[a, slot].wait_recv()
                mine = combine(mine, line_in[turn, a, slot])
        return mine

    def all_gather(turn, block):
        for c in range(COLBLK):
            gathered[turn, 0, 0, c] = block[2 * c : 2 * c + 2]
        line = {}
        for slot in range(depth - 1, 0, -1):
            back = back_of(slot)
            for a in range(CORES if slot >= rim else 1):
                line[a, back] = send(
                    gathered.at[turn, 0, 0, pl.ds(0, COLBLK)],
                    gathered.at[turn, a, 0, pl.ds(back * COLBLK, COLBLK)],
                    back_line_sem.at[turn, a, 0, slot],
                    back_line_sem.at[turn, a, 1, back],
                    cross_peer[slot] if a else line_peer[offset_of(slot, depth)],
                )
        drain(len(line))
        sent = []
        for n, (lo, hi) in enumerate(chunks):
            for slot in range(max(lo, 1), hi):
                line[0, slot].wait_recv()
            at = pl.ds(lo * COLBLK, (hi - lo) * COLBLK)
            for i, (a, b) in enumerate(plane):
                sent.append(
                    send(
                        gathered.at[turn, 0, 0, at],
                        gathered.at[turn, a, (RING - b) % RING, at],
                        back_plane_sem.at[turn, 0, n, i],
                        back_plane_sem.at[turn, 1, n, i],
                        plane_peer[a, b],
                    )
                )
        edge = pl.ds(rim * COLBLK, (depth - rim) * COLBLK)
        for slot in range(rim, depth):
            for a in range(CORES):
                line[a, slot].wait_recv()
        for b in range(1, RING):
            sent.append(
                send(
                    gathered.at[turn, :, 0, edge],
                    gathered.at[turn, :, RING - b, edge],
                    back_far_sem.at[turn, 0, b - 1],
                    back_far_sem.at[turn, 1, b - 1],
                    plane_peer[0, b],
                )
            )
        drain(len(sent))
        for copy in sent:
            copy.wait_recv()

    bits = (depth * COLBLK).bit_length() - 1

    def forward(turn):
        def body(step, acc):
            lhs = []
            for u in range(UNROLL):
                t = step * UNROLL + u
                r = index[0, 0, t]
                at = index[0, 2, t]
                side = at >> (bits + 2)
                pair = gathered[turn, side, (at >> bits) & (RING - 1), at & (depth * COLBLK - 1)]
                value = jnp.where(
                    row < ROWBLK,
                    jnp.broadcast_to(pair[0:1], (8, 128)),
                    jnp.broadcast_to(pair[1:2], (8, 128)),
                )
                lhs.append(split_parts(jnp.where(row % ROWBLK == r, value, 0.0)))
            block = flipped[pl.ds(step * UNROLL, UNROLL)].reshape(UNROLL * 128, 128)
            return acc + jnp.dot(
                jnp.concatenate(lhs, axis=1), block, preferred_element_type=F32
            )

        acc = lax.fori_loop(0, ntile // UNROLL, body, jnp.zeros((16, 128), F32))
        return (acc[0:8] + acc[8:16]) * rscale

    def join(a, b):
        top = lax.broadcasted_iota(jnp.int32, a.shape, a.ndim - 2) < 4
        return jnp.where(top, a + b, jnp.maximum(a, b))

    def add(a, b):
        return a + b

    line = reduce_scatter(0, store_wide, wide_out, wide_core, wide_y, wide_far, join)

    def flip_body(step, carry):
        for u in range(UNROLL):
            t = step * UNROLL + u
            flipped[t] = jnp.transpose(tiles[t])
        return carry

    lax.fori_loop(0, ntile // UNROLL, flip_body, 0)
    mine = collect(0, line, join)

    row4 = lax.broadcasted_iota(jnp.int32, (4, 128), 0)
    cscale = lax.rsqrt(
        jnp.where(
            row4 < 2,
            jnp.broadcast_to(mine[4:5], (4, 128)),
            jnp.broadcast_to(mine[5:6], (4, 128)),
        )
    )
    small[5].wait()
    small[6].wait()
    before = primal_rows(x_start)
    scost = primal_rows(cost) * cscale
    primal = jnp.maximum(0.0, before - step_size * (scost - mine[0:4] * cscale))
    all_gather(0, (2.0 * primal - before) * cscale)
    move = (primal - before) ** 2
    dual = jnp.maximum(0.0, start + step_size * (sbound - forward(0)))
    fill_weights(dual * rscale, table)
    turn = (dual - start) ** 2
    steps = jnp.concatenate(
        [
            move[0:2] + move[2:4],
            jnp.sum(turn[0:4], axis=0, keepdims=True),
            jnp.sum(turn[4:8], axis=0, keepdims=True),
        ],
        axis=0,
    )

    lax.fori_loop(0, ntile // UNROLL, adjoint_body, 0)
    line = reduce_scatter(
        1, store_slim, slim_out, slim_core, slim_y, slim_far, add, steps
    )
    mine = collect(1, line, add)
    sums = jnp.sum(mine[4:8], axis=1, keepdims=True) + 1e-06
    omega = jnp.broadcast_to(jnp.sqrt(sums[2:4] / sums[0:2]), (2, 128))
    wide = jnp.concatenate([omega, omega], axis=0)
    after = jnp.maximum(0.0, primal - (step_size / wide) * (scost - mine[0:4] * cscale))
    all_gather(1, (2.0 * after - primal) * cscale)
    for c in range(COLBLK):
        x_out[:, c * 128 : (c + 1) * 128] = after[2 * c : 2 * c + 2]
    pace = jnp.concatenate(
        [
            jnp.broadcast_to(step_size * omega[0:1], (4, 128)),
            jnp.broadcast_to(step_size * omega[1:2], (4, 128)),
        ],
        axis=0,
    )
    last = jnp.maximum(0.0, dual + pace * (sbound - forward(1)))
    for k in range(2):
        for r in range(ROWBLK):
            y_out[k : k + 1, r * 128 : (r + 1) * 128] = last[k * ROWBLK + r : k * ROWBLK + r + 1]
    drain()


HBM = pl.BlockSpec(memory_space=pltpu.HBM)
VMEM = pl.BlockSpec(memory_space=pltpu.VMEM)
SMEM = pl.BlockSpec(memory_space=pltpu.SMEM)


def shards(tiles, tile_row, tile_col, tile_count, cost, bound_vec, x_start, y_start):
    ntile = tiles.shape[1]
    depth = lax.axis_size("band") // PLANE
    dma = pltpu.SemaphoreType.DMA
    nchunk, rim = (2, depth - 3) if depth >= 8 else (1, 1)
    return pl.pallas_call(
        kernel,
        out_shape=(
            jax.ShapeDtypeStruct((2, COLBLK * 128), F32),
            jax.ShapeDtypeStruct((2, ROWBLK * 128), F32),
        ),
        in_specs=[HBM] * 3 + [SMEM] + [HBM] * 4,
        out_specs=(VMEM, VMEM),
        scratch_shapes=[
            pltpu.VMEM((ntile, 128, 128), BF16),
            pltpu.VMEM((ntile, 128, 128), BF16),
            pltpu.VMEM((ROWBLK + 1, 128, 128), F32),
            pltpu.VMEM((ROWBLK * COLBLK + 1, 16, 128), BF16),
            pltpu.VMEM((ntile + 1, 8, 128), F32),
            pltpu.VMEM((CORES, RING, depth, 8, 128), F32),
            pltpu.VMEM((RING, depth, 8, 128), F32),
            pltpu.VMEM((RING - 1, depth, 8, 128), F32),
            pltpu.VMEM((RING - 1, CORES, depth - rim, 8, 128), F32),
            pltpu.VMEM((CORES, RING, depth, 4, 128), F32),
            pltpu.VMEM((RING, depth, 4, 128), F32),
            pltpu.VMEM((RING - 1, depth, 4, 128), F32),
            pltpu.VMEM((RING - 1, CORES, depth - rim, 4, 128), F32),
            pltpu.VMEM((2, 4, 128), F32),
            pltpu.VMEM((2, RING, 4, 128), F32),
            pltpu.VMEM((2, CORES, depth, 8, 128), F32),
            pltpu.VMEM((2, CORES, depth, 8, 128), F32),
            pltpu.VMEM((2, CORES, RING, depth * COLBLK, 2, 128), F32),
            pltpu.VMEM((1, ntile), jnp.int32),
            pltpu.VMEM((1, ntile), jnp.int32),
            pltpu.VMEM((2, COLBLK * 128), F32),
            pltpu.VMEM((1, ROWBLK * 128), F32),
            pltpu.VMEM((2, COLBLK * 128), F32),
            pltpu.VMEM((2, ROWBLK * 128), F32),
            pltpu.SMEM((1, ntile), jnp.int32),
            pltpu.VMEM((2, 8, 128), jnp.int32),
            pltpu.SMEM((2, 8, 128), jnp.int32),
            dma((ntile // PIECE,)),
            dma((8,)),
            dma((2, 2, nchunk)),
            dma((2, 2, nchunk, RING - 1)),
            dma((2, 2, RING - 1)),
            dma((2, 2, RING)),
            dma((2, CORES, 2, depth)),
            dma((2, CORES, 2, depth)),
            dma((2, 2, nchunk, PLANE - 1)),
            dma((2, 2, RING - 1)),
        ],
        compiler_params=pltpu.CompilerParams(
            collective_id=0, has_side_effects=True, vmem_limit_bytes=60 << 20
        ),
    )(
        tiles,
        tile_row,
        tile_col,
        tile_count,
        cost,
        bound_vec.reshape(1, -1),
        x_start,
        y_start,
    )


def solution(mesh):
    return jax.shard_map(
        shards,
        mesh=mesh,
        in_specs=(
            P("band", None, None, None),
            P("band", None),
            P("band", None),
            P("band"),
            P("batch", "band"),
            P("band"),
            P("batch", "band"),
            P("batch", "band"),
        ),
        out_specs=(P("batch", "band"), P("batch", "band")),
        check_vma=False,
    )
```

```python
import jax
import jax.numpy as jnp
from jax import lax
from jax.experimental import pallas as pl
from jax.experimental.pallas import tpu as pltpu
from jax.sharding import PartitionSpec as P

ROWBLK = 4
COLBLK = 2
CORES = 2
RING = 4
PLANE = CORES * RING
UNROLL = 64
PIECE = 64

step_size = 0.0625
MESH = pl.DeviceIdType.MESH
F32 = jnp.float32
BF16 = jnp.bfloat16


def rows8():
    return lax.broadcasted_iota(jnp.int32, (8, 128), 0)


def split_parts(value):
    high = value.astype(BF16).astype(F32)
    return jnp.concatenate([high, value - high], axis=0).astype(BF16)


def slot_of(offset, depth):
    if isinstance(offset, int):
        return max(2 * offset - 1, 0) if offset <= depth // 2 else 2 * (depth - offset)
    ahead = jnp.maximum(2 * offset - 1, 0)
    return jnp.where(offset <= depth // 2, ahead, 2 * (depth - offset))


def offset_of(slot, depth):
    return (slot + 1) // 2 if slot % 2 == 1 else (depth - slot // 2) % depth


def dual_rows(ref):
    return jnp.concatenate(
        [ref[k : k + 1, r * 128 : (r + 1) * 128] for k in range(2) for r in range(ROWBLK)], axis=0
    )


def bound_rows(ref):
    rows = [ref[0:1, r * 128 : (r + 1) * 128] for r in range(ROWBLK)]
    return jnp.concatenate(rows + rows, axis=0)


def primal_rows(ref):
    return jnp.concatenate(
        [ref[k : k + 1, c * 128 : (c + 1) * 128] for c in range(COLBLK) for k in range(2)], axis=0
    )


def fill_weights(weighted, table):
    row = rows8()
    for r in range(ROWBLK):
        first = jnp.broadcast_to(weighted[r : r + 1], (8, 128))
        second = jnp.broadcast_to(weighted[ROWBLK + r : ROWBLK + r + 1], (8, 128))
        for c in range(COLBLK):
            entry = jnp.where(row == 2 * c, first, jnp.where(row == 2 * c + 1, second, 0.0))
            table[r * COLBLK + c] = split_parts(entry)
    table[ROWBLK * COLBLK] = jnp.zeros((16, 128), BF16)


def fill_index(rows, cols, count, depth, y, z, core, index):
    ntile = rows.shape[1]
    lane = lax.broadcasted_iota(jnp.int32, (8, ntile), 1)
    live = lane < count
    row = jnp.broadcast_to(rows, (8, ntile))
    col = jnp.broadcast_to(cols, (8, ntile))
    part = col & 1
    owner = col >> 1
    side = (owner + core) & 1
    turn = ((owner >> 1) + RING - y) & (RING - 1)
    far = ((owner >> 3) + depth - z) & (depth - 1)
    slot = jnp.where(far <= depth // 2, jnp.maximum(2 * far - 1, 0), 2 * (depth - far))
    place = (side * RING + turn) * depth + slot
    at = lax.broadcasted_iota(jnp.int32, (8, ntile), 0)
    index[0, :, 0:ntile] = jnp.where(
        at == 0,
        jnp.where(live, row, ROWBLK),
        jnp.where(
            at == 1,
            jnp.where(live, row * COLBLK + part, ROWBLK * COLBLK),
            place * COLBLK + part,
        ),
    )
    places = PLANE * depth
    wide = jnp.broadcast_to(jnp.where(live, place, -1)[0:1], (128, ntile)).astype(F32)
    match = jnp.transpose(wide) == lax.broadcasted_iota(jnp.int32, (ntile, 128), 1).astype(F32)
    tile = lax.broadcasted_iota(jnp.int32, (ntile, 128), 0)
    first = jnp.min(jnp.where(match, tile, ntile), axis=0, keepdims=True)
    second = jnp.max(jnp.where(match, tile, -1), axis=0, keepdims=True)
    second = jnp.where(second > first, second, ntile)
    at = lax.broadcasted_iota(jnp.int32, (8, 128), 0)
    index[1] = jnp.where(
        at == 0, jnp.broadcast_to(first, (8, 128)), jnp.broadcast_to(second, (8, 128))
    )


def kernel(
    tiles_in,
    row_in,
    col_in,
    tile_count,
    cost_in,
    bound_in,
    x_in,
    y_in,
    x_out,
    y_out,
    tiles,
    flipped,
    spread,
    table,
    parts,
    wide_out,
    wide_core,
    wide_y,
    wide_far,
    slim_out,
    slim_core,
    slim_y,
    slim_far,
    steps_out,
    steps_in,
    reduced,
    line_in,
    gathered,
    row_vmem,
    col_vmem,
    cost,
    bound_vec,
    x_start,
    y_start,
    tile_row,
    index_vmem,
    index,
    tile_sem,
    small_sem,
    core_sem,
    ring_sem,
    far_sem,
    steps_sem,
    line_sem,
    back_line_sem,
    back_plane_sem,
    back_far_sem,
):
    ntile = tiles.shape[0]
    depth = reduced.shape[2]
    edges = (0, depth // 2 + 1, depth - 3) if depth >= 8 else (0, 1)
    chunks = tuple(zip(edges[:-1], edges[1:]))
    nchunk = len(chunks)
    rim = edges[-1]
    far = pl.ds(rim, depth - rim)
    me = lax.axis_index("band")
    z = me // PLANE
    y = (me // CORES) % RING
    core = me % CORES
    plane = [(a, b) for a in range(CORES) for b in range(RING) if (a, b) != (0, 0)]
    plane_peer = {
        (a, b): z * PLANE + ((y + b) % RING) * CORES + (core + a) % CORES for a, b in plane
    }
    line_peer = {d: ((z + d) % depth) * PLANE + me % PLANE for d in range(1, depth)}
    cross_peer = {
        slot: ((z + offset_of(slot, depth)) % depth) * PLANE + me % PLANE + 1 - 2 * core
        for slot in range(rim, depth)
    }
    peers = list(plane_peer.values()) + list(line_peer.values()) + list(cross_peer.values())
    count = tile_count[0]
    row = rows8()
    started = []

    barrier = pltpu.get_barrier_semaphore()
    for band in peers:
        pl.semaphore_signal(barrier, inc=1, device_id={"band": band}, device_id_type=MESH)

    def piece_copy(i):
        at = pl.ds(i * PIECE, PIECE)
        return pltpu.make_async_copy(tiles_in.at[0, at], tiles.at[at], tile_sem.at[i])

    small = [
        pltpu.make_async_copy(src, dst, small_sem.at[i])
        for i, (src, dst) in enumerate(
            (
                (row_in, tile_row),
                (row_in, row_vmem),
                (col_in, col_vmem),
                (y_in, y_start),
                (bound_in, bound_vec),
                (x_in, x_start),
                (cost_in, cost),
            )
        )
    ]
    index_copy = pltpu.make_async_copy(index_vmem, index, small_sem.at[len(small)])
    for copy in small[:3]:
        copy.start()
    for i in range(ntile // PIECE):
        piece_copy(i).start()
    for copy in small[3:]:
        copy.start()
    small[1].wait()
    small[2].wait()
    fill_index(row_vmem[...], col_vmem[...], count, depth, y, z, core, index_vmem)
    index_copy.start()
    small[0].wait()

    def send(src, dst, send_sem, recv_sem, band):
        copy = pltpu.make_async_remote_copy(
            src_ref=src,
            dst_ref=dst,
            send_sem=send_sem,
            recv_sem=recv_sem,
            device_id={"band": band},
            device_id_type=MESH,
        )
        copy.start()
        started.append(copy)
        return copy

    def drain(kept=0):
        done = started[: len(started) - kept]
        del started[: len(done)]
        for copy in done:
            copy.wait_send()

    def live_row(t):
        return jnp.where(t < count, tile_row[0, t], ROWBLK)

    def peak_piece(i, peaks):
        piece_copy(i).wait()

        def peak_body(step, peaks):
            peaks = list(peaks)
            for u in range(UNROLL):
                t = i * PIECE + step * UNROLL + u
                r = live_row(t)
                size = jnp.abs(tiles[t])
                for k in range(ROWBLK):
                    peaks[k] = jnp.maximum(peaks[k], jnp.where(r == k, size, jnp.zeros_like(size)))
            return tuple(peaks)

        return lax.fori_loop(0, PIECE // UNROLL, peak_body, peaks)

    peaks = lax.fori_loop(
        0, ntile // PIECE, peak_piece, (jnp.zeros((128, 128), BF16),) * ROWBLK
    )
    lines = []
    for r in range(ROWBLK):
        peak = jnp.max(peaks[r].astype(F32), axis=1, keepdims=True)
        scale = jnp.broadcast_to(lax.rsqrt(peak), (128, 128))
        spread[r] = scale
        lines.append(jnp.transpose(scale)[0:1])
    spread[ROWBLK] = jnp.zeros((128, 128), F32)
    rscale = jnp.concatenate(lines + lines, axis=0)
    small[3].wait()
    small[4].wait()
    start = dual_rows(y_start)
    sbound = bound_rows(bound_vec) * rscale
    fill_weights(start * rscale, table)
    parts[ntile] = jnp.zeros((8, 128), F32)
    index_copy.wait()

    def scale_body(step, carry):
        for u in range(UNROLL):
            t = step * UNROLL + u
            entry = index[0, 1, t]
            block = tiles[t]
            peak = jnp.max(
                jnp.abs(block.astype(F32)) * spread[index[0, 0, t]], axis=0, keepdims=True
            )
            peak = jnp.broadcast_to(peak, (8, 128))
            product = jnp.dot(table[entry], block, preferred_element_type=F32)
            parts[t] = jnp.where(
                row < 4,
                product[0:8] + product[8:16],
                jnp.where(row == 4 + (entry & 1), peak, 0.0),
            )
        return carry

    lax.fori_loop(0, ntile // UNROLL, scale_body, 0)

    def adjoint_body(step, carry):
        for u in range(UNROLL):
            t = step * UNROLL + u
            product = jnp.dot(table[index[0, 1, t]], tiles[t], preferred_element_type=F32)
            parts[t] = product[0:8] + product[8:16]
        return carry

    def place_parts(store, lo, hi):
        def body(slot, carry):
            for a in range(CORES):
                for b in range(RING):
                    at = (a * RING + b) * depth + slot
                    store(a, b, slot, parts[index[1, 0, at]], parts[index[1, 1, at]])
            return carry

        lax.fori_loop(lo, hi, body, 0)

    def store_wide(a, b, slot, first, second):
        wide_out[a, b, slot] = jnp.where(row < 4, first + second, jnp.maximum(first, second))

    def store_slim(a, b, slot, first, second):
        slim_out[a, b, slot] = (first + second)[0:4]

    def back_of(slot):
        return slot_of((depth - offset_of(slot, depth)) % depth, depth)

    def reduce_scatter(turn, store, out, from_core, from_y, from_far, combine, steps=None):
        order = tuple(range(nchunk))[::-1]
        used = pl.ds(0, 4 if steps is not None else 6)
        sent = {}

        def send_steps(kind, b):
            sent["steps", kind, b] = send(
                steps_out.at[kind],
                steps_in.at[kind, b],
                steps_sem.at[0, kind, b],
                steps_sem.at[1, kind, b],
                plane_peer[0, b] if b else plane_peer[1, 0],
            )

        place_parts(store, rim, depth)
        if steps is not None:
            steps_out[0] = steps
            for b in range(RING):
                send_steps(0, b)
        else:
            pl.semaphore_wait(barrier, len(peers))
        for b in range(1, RING):
            sent["far", b] = send(
                out.at[:, b, far, used],
                from_far.at[b - 1, :, :, used],
                far_sem.at[turn, 0, b - 1],
                far_sem.at[turn, 1, b - 1],
                plane_peer[0, b],
            )
        for n in order:
            at = pl.ds(chunks[n][0], chunks[n][1] - chunks[n][0])
            place_parts(store, *chunks[n])
            sent[n] = send(
                out.at[1, :, at, used],
                from_core.at[:, at, used],
                core_sem.at[turn, 0, n],
                core_sem.at[turn, 1, n],
                plane_peer[1, 0],
            )
        if steps is not None:
            sent["steps", 0, 0].wait_recv()
            both = steps + steps_in[0, 0]
            steps_out[1] = both
            for b in range(1, RING):
                send_steps(1, b)
        for n in order:
            lo, hi = chunks[n]
            at = pl.ds(lo, hi - lo)
            sent[n].wait_recv()
            for b in range(RING):
                from_core[b, lo:hi] = combine(out[0, b, lo:hi], from_core[b, lo:hi])
            for b in range(1, RING):
                sent[n, b] = send(
                    from_core.at[b, at, used],
                    from_y.at[b - 1, at, used],
                    ring_sem.at[turn, 0, n, b - 1],
                    ring_sem.at[turn, 1, n, b - 1],
                    plane_peer[0, b],
                )

        def keep(a, lo, hi, total, extra):
            if extra is None:
                reduced[turn, a, lo:hi] = total
            else:
                reduced[turn, a, lo:hi, 0:4] = total
                reduced[turn, a, lo:hi, 4:8] = jnp.broadcast_to(extra[None], (hi - lo, 4, 128))

        if steps is not None:
            for b in range(1, RING):
                sent["steps", 0, b].wait_recv()
                steps = steps + steps_in[0, b]
        for b in range(1, RING):
            sent["far", b].wait_recv()
        for a in range(CORES):
            total = out[a, 0, rim:depth]
            for b in range(1, RING):
                total = combine(total, from_far[b - 1, a])
            keep(a, rim, depth, total, steps)
        line = {}

        def along(a, slot):
            back = back_of(slot)
            line[a, back] = send(
                reduced.at[turn, a, slot],
                line_in.at[turn, a, back],
                line_sem.at[turn, a, 0, slot],
                line_sem.at[turn, a, 1, back],
                cross_peer[slot] if a else line_peer[offset_of(slot, depth)],
            )

        for slot in range(depth - 1, rim - 1, -1):
            for a in range(CORES):
                along(a, slot)
        if steps is not None:
            for b in range(1, RING):
                sent["steps", 1, b].wait_recv()
                both = both + steps_in[1, b]
            steps = both
        for n in order:
            lo, hi = chunks[n]
            total = from_core[0, lo:hi]
            for b in range(1, RING):
                sent[n, b].wait_recv()
                total = combine(total, from_y[b - 1, lo:hi])
            keep(0, lo, hi, total, steps)
            for slot in range(hi - 1, max(lo, 1) - 1, -1):
                along(0, slot)
        return line

    def collect(turn, line, combine):
        mine = reduced[turn, 0, 0]
        for slot in range(1, depth):
            for a in range(CORES if slot >= rim else 1):
                line[a, slot].wait_recv()
                mine = combine(mine, line_in[turn, a, slot])
        return mine

    def all_gather(turn, block):
        for c in range(COLBLK):
            gathered[turn, 0, 0, c] = block[2 * c : 2 * c + 2]
        line = {}
        for slot in range(depth - 1, 0, -1):
            back = back_of(slot)
            for a in range(CORES if slot >= rim else 1):
                line[a, back] = send(
                    gathered.at[turn, 0, 0, pl.ds(0, COLBLK)],
                    gathered.at[turn, a, 0, pl.ds(back * COLBLK, COLBLK)],
                    back_line_sem.at[turn, a, 0, slot],
                    back_line_sem.at[turn, a, 1, back],
                    cross_peer[slot] if a else line_peer[offset_of(slot, depth)],
                )
        drain(len(line))
        sent = []
        for n, (lo, hi) in enumerate(chunks):
            for slot in range(max(lo, 1), hi):
                line[0, slot].wait_recv()
            at = pl.ds(lo * COLBLK, (hi - lo) * COLBLK)
            for i, (a, b) in enumerate(plane):
                sent.append(
                    send(
                        gathered.at[turn, 0, 0, at],
                        gathered.at[turn, a, (RING - b) % RING, at],
                        back_plane_sem.at[turn, 0, n, i],
                        back_plane_sem.at[turn, 1, n, i],
                        plane_peer[a, b],
                    )
                )
        edge = pl.ds(rim * COLBLK, (depth - rim) * COLBLK)
        for slot in range(rim, depth):
            for a in range(CORES):
                line[a, slot].wait_recv()
        for b in range(1, RING):
            sent.append(
                send(
                    gathered.at[turn, :, 0, edge],
                    gathered.at[turn, :, RING - b, edge],
                    back_far_sem.at[turn, 0, b - 1],
                    back_far_sem.at[turn, 1, b - 1],
                    plane_peer[0, b],
                )
            )
        drain(len(sent))
        for copy in sent:
            copy.wait_recv()

    bits = (depth * COLBLK).bit_length() - 1

    def forward(turn):
        def body(step, acc):
            lhs = []
            for u in range(UNROLL):
                t = step * UNROLL + u
                r = index[0, 0, t]
                at = index[0, 2, t]
                side = at >> (bits + 2)
                pair = gathered[turn, side, (at >> bits) & (RING - 1), at & (depth * COLBLK - 1)]
                value = jnp.where(
                    row < ROWBLK,
                    jnp.broadcast_to(pair[0:1], (8, 128)),
                    jnp.broadcast_to(pair[1:2], (8, 128)),
                )
                lhs.append(split_parts(jnp.where(row % ROWBLK == r, value, 0.0)))
            block = flipped[pl.ds(step * UNROLL, UNROLL)].reshape(UNROLL * 128, 128)
            return acc + jnp.dot(
                jnp.concatenate(lhs, axis=1), block, preferred_element_type=F32
            )

        acc = lax.fori_loop(0, ntile // UNROLL, body, jnp.zeros((16, 128), F32))
        return (acc[0:8] + acc[8:16]) * rscale

    def join(a, b):
        top = lax.broadcasted_iota(jnp.int32, a.shape, a.ndim - 2) < 4
        return jnp.where(top, a + b, jnp.maximum(a, b))

    def add(a, b):
        return a + b

    line = reduce_scatter(0, store_wide, wide_out, wide_core, wide_y, wide_far, join)

    def flip_body(step, carry):
        for u in range(UNROLL):
            t = step * UNROLL + u
            flipped[t] = jnp.transpose(tiles[t])
        return carry

    lax.fori_loop(0, ntile // UNROLL, flip_body, 0)
    mine = collect(0, line, join)

    row4 = lax.broadcasted_iota(jnp.int32, (4, 128), 0)
    cscale = lax.rsqrt(
        jnp.where(
            row4 < 2,
            jnp.broadcast_to(mine[4:5], (4, 128)),
            jnp.broadcast_to(mine[5:6], (4, 128)),
        )
    )
    small[5].wait()
    small[6].wait()
    before = primal_rows(x_start)
    scost = primal_rows(cost) * cscale
    primal = jnp.maximum(0.0, before - step_size * (scost - mine[0:4] * cscale))
    all_gather(0, (2.0 * primal - before) * cscale)
    move = (primal - before) ** 2
    dual = jnp.maximum(0.0, start + step_size * (sbound - forward(0)))
    fill_weights(dual * rscale, table)
    turn = (dual - start) ** 2
    steps = jnp.concatenate(
        [
            move[0:2] + move[2:4],
            jnp.sum(turn[0:4], axis=0, keepdims=True),
            jnp.sum(turn[4:8], axis=0, keepdims=True),
        ],
        axis=0,
    )

    lax.fori_loop(0, ntile // UNROLL, adjoint_body, 0)
    line = reduce_scatter(
        1, store_slim, slim_out, slim_core, slim_y, slim_far, add, steps
    )
    mine = collect(1, line, add)
    sums = jnp.sum(mine[4:8], axis=1, keepdims=True) + 1e-06
    omega = jnp.broadcast_to(jnp.sqrt(sums[2:4] / sums[0:2]), (2, 128))
    wide = jnp.concatenate([omega, omega], axis=0)
    after = jnp.maximum(0.0, primal - (step_size / wide) * (scost - mine[0:4] * cscale))
    all_gather(1, (2.0 * after - primal) * cscale)
    for c in range(COLBLK):
        x_out[:, c * 128 : (c + 1) * 128] = after[2 * c : 2 * c + 2]
    pace = jnp.concatenate(
        [
            jnp.broadcast_to(step_size * omega[0:1], (4, 128)),
            jnp.broadcast_to(step_size * omega[1:2], (4, 128)),
        ],
        axis=0,
    )
    last = jnp.maximum(0.0, dual + pace * (sbound - forward(1)))
    for k in range(2):
        for r in range(ROWBLK):
            y_out[k : k + 1, r * 128 : (r + 1) * 128] = last[k * ROWBLK + r : k * ROWBLK + r + 1]
    drain()


HBM = pl.BlockSpec(memory_space=pltpu.HBM)
VMEM = pl.BlockSpec(memory_space=pltpu.VMEM)
SMEM = pl.BlockSpec(memory_space=pltpu.SMEM)


def shards(tiles, tile_row, tile_col, tile_count, cost, bound_vec, x_start, y_start):
    ntile = tiles.shape[1]
    depth = lax.axis_size("band") // PLANE
    dma = pltpu.SemaphoreType.DMA
    nchunk, rim = (2, depth - 3) if depth >= 8 else (1, 1)
    return pl.pallas_call(
        kernel,
        out_shape=(
            jax.ShapeDtypeStruct((2, COLBLK * 128), F32),
            jax.ShapeDtypeStruct((2, ROWBLK * 128), F32),
        ),
        in_specs=[HBM] * 3 + [SMEM] + [HBM] * 4,
        out_specs=(VMEM, VMEM),
        scratch_shapes=[
            pltpu.VMEM((ntile, 128, 128), BF16),
            pltpu.VMEM((ntile, 128, 128), BF16),
            pltpu.VMEM((ROWBLK + 1, 128, 128), F32),
            pltpu.VMEM((ROWBLK * COLBLK + 1, 16, 128), BF16),
            pltpu.VMEM((ntile + 1, 8, 128), F32),
            pltpu.VMEM((CORES, RING, depth, 8, 128), F32),
            pltpu.VMEM((RING, depth, 8, 128), F32),
            pltpu.VMEM((RING - 1, depth, 8, 128), F32),
            pltpu.VMEM((RING - 1, CORES, depth - rim, 8, 128), F32),
            pltpu.VMEM((CORES, RING, depth, 4, 128), F32),
            pltpu.VMEM((RING, depth, 4, 128), F32),
            pltpu.VMEM((RING - 1, depth, 4, 128), F32),
            pltpu.VMEM((RING - 1, CORES, depth - rim, 4, 128), F32),
            pltpu.VMEM((2, 4, 128), F32),
            pltpu.VMEM((2, RING, 4, 128), F32),
            pltpu.VMEM((2, CORES, depth, 8, 128), F32),
            pltpu.VMEM((2, CORES, depth, 8, 128), F32),
            pltpu.VMEM((2, CORES, RING, depth * COLBLK, 2, 128), F32),
            pltpu.VMEM((1, ntile), jnp.int32),
            pltpu.VMEM((1, ntile), jnp.int32),
            pltpu.VMEM((2, COLBLK * 128), F32),
            pltpu.VMEM((1, ROWBLK * 128), F32),
            pltpu.VMEM((2, COLBLK * 128), F32),
            pltpu.VMEM((2, ROWBLK * 128), F32),
            pltpu.SMEM((1, ntile), jnp.int32),
            pltpu.VMEM((2, 8, 128), jnp.int32),
            pltpu.SMEM((2, 8, 128), jnp.int32),
            dma((ntile // PIECE,)),
            dma((8,)),
            dma((2, 2, nchunk)),
            dma((2, 2, nchunk, RING - 1)),
            dma((2, 2, RING - 1)),
            dma((2, 2, RING)),
            dma((2, CORES, 2, depth)),
            dma((2, CORES, 2, depth)),
            dma((2, 2, nchunk, PLANE - 1)),
            dma((2, 2, RING - 1)),
        ],
        compiler_params=pltpu.CompilerParams(
            collective_id=0, has_side_effects=True, vmem_limit_bytes=60 << 20
        ),
    )(
        tiles,
        tile_row,
        tile_col,
        tile_count,
        cost,
        bound_vec.reshape(1, -1),
        x_start,
        y_start,
    )


def solution(mesh):
    return jax.shard_map(
        shards,
        mesh=mesh,
        in_specs=(
            P("band", None, None, None),
            P("band", None),
            P("band", None),
            P("band"),
            P("batch", "band"),
            P("band"),
            P("batch", "band"),
            P("batch", "band"),
        ),
        out_specs=(P("batch", "band"), P("batch", "band")),
        check_vma=False,
    )
```

```python
import jax
import jax.numpy as jnp
from jax import lax
from jax.experimental import pallas as pl
from jax.experimental.pallas import tpu as pltpu
from jax.sharding import PartitionSpec as P

ROWBLK = 4
COLBLK = 2
CORES = 2
RING = 4
PLANE = CORES * RING
UNROLL = 64
PIECE = 16

step_size = 0.0625
MESH = pl.DeviceIdType.MESH
F32 = jnp.float32
BF16 = jnp.bfloat16


def rows8():
    return lax.broadcasted_iota(jnp.int32, (8, 128), 0)


def split_parts(value):
    high = value.astype(BF16).astype(F32)
    return jnp.concatenate([high, value - high], axis=0).astype(BF16)


def slot_of(offset, depth):
    if isinstance(offset, int):
        return max(2 * offset - 1, 0) if offset <= depth // 2 else 2 * (depth - offset)
    ahead = jnp.maximum(2 * offset - 1, 0)
    return jnp.where(offset <= depth // 2, ahead, 2 * (depth - offset))


def offset_of(slot, depth):
    return (slot + 1) // 2 if slot % 2 == 1 else (depth - slot // 2) % depth


def dual_rows(ref):
    return jnp.concatenate(
        [ref[k : k + 1, r * 128 : (r + 1) * 128] for k in range(2) for r in range(ROWBLK)], axis=0
    )


def bound_rows(ref):
    rows = [ref[0:1, r * 128 : (r + 1) * 128] for r in range(ROWBLK)]
    return jnp.concatenate(rows + rows, axis=0)


def primal_rows(ref):
    return jnp.concatenate(
        [ref[k : k + 1, c * 128 : (c + 1) * 128] for c in range(COLBLK) for k in range(2)], axis=0
    )


def fill_weights(weighted, table):
    row = rows8()
    for r in range(ROWBLK):
        first = jnp.broadcast_to(weighted[r : r + 1], (8, 128))
        second = jnp.broadcast_to(weighted[ROWBLK + r : ROWBLK + r + 1], (8, 128))
        for c in range(COLBLK):
            entry = jnp.where(row == 2 * c, first, jnp.where(row == 2 * c + 1, second, 0.0))
            table[r * COLBLK + c] = split_parts(entry)
    table[ROWBLK * COLBLK] = jnp.zeros((16, 128), BF16)


def fill_index(rows, cols, count, depth, y, z, core, index):
    ntile = rows.shape[1]
    lane = lax.broadcasted_iota(jnp.int32, (8, ntile), 1)
    live = lane < count
    row = jnp.broadcast_to(rows, (8, ntile))
    col = jnp.broadcast_to(cols, (8, ntile))
    part = col & 1
    owner = col >> 1
    side = (owner + core) & 1
    turn = ((owner >> 1) + RING - y) & (RING - 1)
    far = ((owner >> 3) + depth - z) & (depth - 1)
    slot = jnp.where(far <= depth // 2, jnp.maximum(2 * far - 1, 0), 2 * (depth - far))
    place = (side * RING + turn) * depth + slot
    at = lax.broadcasted_iota(jnp.int32, (8, ntile), 0)
    index[0, :, 0:ntile] = jnp.where(
        at == 0,
        jnp.where(live, row, ROWBLK),
        jnp.where(
            at == 1,
            jnp.where(live, row * COLBLK + part, ROWBLK * COLBLK),
            place * COLBLK + part,
        ),
    )
    places = PLANE * depth
    wide = jnp.broadcast_to(jnp.where(live, place, -1)[0:1], (128, ntile)).astype(F32)
    match = jnp.transpose(wide) == lax.broadcasted_iota(jnp.int32, (ntile, 128), 1).astype(F32)
    tile = lax.broadcasted_iota(jnp.int32, (ntile, 128), 0)
    first = jnp.min(jnp.where(match, tile, ntile), axis=0, keepdims=True)
    second = jnp.max(jnp.where(match, tile, -1), axis=0, keepdims=True)
    second = jnp.where(second > first, second, ntile)
    at = lax.broadcasted_iota(jnp.int32, (8, 128), 0)
    index[1] = jnp.where(
        at == 0, jnp.broadcast_to(first, (8, 128)), jnp.broadcast_to(second, (8, 128))
    )


def kernel(
    tiles_in,
    row_in,
    col_in,
    tile_count,
    cost_in,
    bound_in,
    x_in,
    y_in,
    x_out,
    y_out,
    tiles,
    flipped,
    spread,
    table,
    parts,
    wide_out,
    wide_core,
    wide_y,
    wide_far,
    slim_out,
    slim_core,
    slim_y,
    slim_far,
    steps_out,
    steps_in,
    reduced,
    line_in,
    gathered,
    row_vmem,
    col_vmem,
    cost,
    bound_vec,
    x_start,
    y_start,
    tile_row,
    index_vmem,
    index,
    tile_sem,
    small_sem,
    core_sem,
    ring_sem,
    far_sem,
    steps_sem,
    line_sem,
    back_line_sem,
    back_plane_sem,
    back_far_sem,
):
    ntile = tiles.shape[0]
    depth = reduced.shape[2]
    edges = (0, depth // 2 + 1, depth - 3) if depth >= 8 else (0, 1)
    chunks = tuple(zip(edges[:-1], edges[1:]))
    nchunk = len(chunks)
    rim = edges[-1]
    far = pl.ds(rim, depth - rim)
    me = lax.axis_index("band")
    z = me // PLANE
    y = (me // CORES) % RING
    core = me % CORES
    plane = [(a, b) for a in range(CORES) for b in range(RING) if (a, b) != (0, 0)]
    plane_peer = {
        (a, b): z * PLANE + ((y + b) % RING) * CORES + (core + a) % CORES for a, b in plane
    }
    line_peer = {d: ((z + d) % depth) * PLANE + me % PLANE for d in range(1, depth)}
    cross_peer = {
        slot: ((z + offset_of(slot, depth)) % depth) * PLANE + me % PLANE + 1 - 2 * core
        for slot in range(rim, depth)
    }
    peers = list(plane_peer.values()) + list(line_peer.values()) + list(cross_peer.values())
    count = tile_count[0]
    row = rows8()
    started = []

    barrier = pltpu.get_barrier_semaphore()
    for band in peers:
        pl.semaphore_signal(barrier, inc=1, device_id={"band": band}, device_id_type=MESH)

    def piece_copy(i):
        at = pl.ds(i * PIECE, PIECE)
        return pltpu.make_async_copy(tiles_in.at[0, at], tiles.at[at], tile_sem.at[i])

    small = [
        pltpu.make_async_copy(src, dst, small_sem.at[i])
        for i, (src, dst) in enumerate(
            (
                (row_in, tile_row),
                (row_in, row_vmem),
                (col_in, col_vmem),
                (y_in, y_start),
                (bound_in, bound_vec),
                (x_in, x_start),
                (cost_in, cost),
            )
        )
    ]
    index_copy = pltpu.make_async_copy(index_vmem, index, small_sem.at[len(small)])
    for copy in small[:3]:
        copy.start()
    for i in range(ntile // PIECE):
        piece_copy(i).start()
    for copy in small[3:]:
        copy.start()
    small[1].wait()
    small[2].wait()
    fill_index(row_vmem[...], col_vmem[...], count, depth, y, z, core, index_vmem)
    index_copy.start()
    small[0].wait()

    def send(src, dst, send_sem, recv_sem, band):
        copy = pltpu.make_async_remote_copy(
            src_ref=src,
            dst_ref=dst,
            send_sem=send_sem,
            recv_sem=recv_sem,
            device_id={"band": band},
            device_id_type=MESH,
        )
        copy.start()
        started.append(copy)
        return copy

    def drain(kept=0):
        done = started[: len(started) - kept]
        del started[: len(done)]
        for copy in done:
            copy.wait_send()

    def live_row(t):
        return jnp.where(t < count, tile_row[0, t], ROWBLK)

    def peak_piece(i, peaks):
        piece_copy(i).wait()

        def peak_body(peaks):
            peaks = list(peaks)
            for u in range(PIECE):
                t = i * PIECE + u
                r = live_row(t)
                size = jnp.abs(tiles[t])
                for k in range(ROWBLK):
                    peaks[k] = jnp.maximum(peaks[k], jnp.where(r == k, size, jnp.zeros_like(size)))
            return tuple(peaks)

        return peak_body(peaks)

    peaks = lax.fori_loop(
        0, ntile // PIECE, peak_piece, (jnp.zeros((128, 128), BF16),) * ROWBLK
    )
    lines = []
    for r in range(ROWBLK):
        peak = jnp.max(peaks[r].astype(F32), axis=1, keepdims=True)
        scale = jnp.broadcast_to(lax.rsqrt(peak), (128, 128))
        spread[r] = scale
        lines.append(jnp.transpose(scale)[0:1])
    spread[ROWBLK] = jnp.zeros((128, 128), F32)
    rscale = jnp.concatenate(lines + lines, axis=0)
    small[3].wait()
    small[4].wait()
    start = dual_rows(y_start)
    sbound = bound_rows(bound_vec) * rscale
    fill_weights(start * rscale, table)
    parts[ntile] = jnp.zeros((8, 128), F32)
    index_copy.wait()

    def scale_body(step, carry):
        for u in range(UNROLL):
            t = step * UNROLL + u
            entry = index[0, 1, t]
            block = tiles[t]
            peak = jnp.max(
                jnp.abs(block.astype(F32)) * spread[index[0, 0, t]], axis=0, keepdims=True
            )
            peak = jnp.broadcast_to(peak, (8, 128))
            product = jnp.dot(table[entry], block, preferred_element_type=F32)
            parts[t] = jnp.where(
                row < 4,
                product[0:8] + product[8:16],
                jnp.where(row == 4 + (entry & 1), peak, 0.0),
            )
        return carry

    lax.fori_loop(0, ntile // UNROLL, scale_body, 0)

    def adjoint_body(step, carry):
        for u in range(UNROLL):
            t = step * UNROLL + u
            product = jnp.dot(table[index[0, 1, t]], tiles[t], preferred_element_type=F32)
            parts[t] = product[0:8] + product[8:16]
        return carry

    def place_parts(store, lo, hi):
        def body(slot, carry):
            for a in range(CORES):
                for b in range(RING):
                    at = (a * RING + b) * depth + slot
                    store(a, b, slot, parts[index[1, 0, at]], parts[index[1, 1, at]])
            return carry

        lax.fori_loop(lo, hi, body, 0)

    def store_wide(a, b, slot, first, second):
        wide_out[a, b, slot] = jnp.where(row < 4, first + second, jnp.maximum(first, second))

    def store_slim(a, b, slot, first, second):
        slim_out[a, b, slot] = (first + second)[0:4]

    def back_of(slot):
        return slot_of((depth - offset_of(slot, depth)) % depth, depth)

    def reduce_scatter(turn, store, out, from_core, from_y, from_far, combine, steps=None):
        order = tuple(range(nchunk))[::-1]
        used = pl.ds(0, 4 if steps is not None else 6)
        sent = {}

        def send_steps(kind, b):
            sent["steps", kind, b] = send(
                steps_out.at[kind],
                steps_in.at[kind, b],
                steps_sem.at[0, kind, b],
                steps_sem.at[1, kind, b],
                plane_peer[0, b] if b else plane_peer[1, 0],
            )

        place_parts(store, rim, depth)
        if steps is not None:
            steps_out[0] = steps
            for b in range(RING):
                send_steps(0, b)
        else:
            pl.semaphore_wait(barrier, len(peers))
        for b in range(1, RING):
            sent["far", b] = send(
                out.at[:, b, far, used],
                from_far.at[b - 1, :, :, used],
                far_sem.at[turn, 0, b - 1],
                far_sem.at[turn, 1, b - 1],
                plane_peer[0, b],
            )
        for n in order:
            at = pl.ds(chunks[n][0], chunks[n][1] - chunks[n][0])
            place_parts(store, *chunks[n])
            sent[n] = send(
                out.at[1, :, at, used],
                from_core.at[:, at, used],
                core_sem.at[turn, 0, n],
                core_sem.at[turn, 1, n],
                plane_peer[1, 0],
            )
        if steps is not None:
            sent["steps", 0, 0].wait_recv()
            both = steps + steps_in[0, 0]
            steps_out[1] = both
            for b in range(1, RING):
                send_steps(1, b)
        for n in order:
            lo, hi = chunks[n]
            at = pl.ds(lo, hi - lo)
            sent[n].wait_recv()
            for b in range(RING):
                from_core[b, lo:hi] = combine(out[0, b, lo:hi], from_core[b, lo:hi])
            for b in range(1, RING):
                sent[n, b] = send(
                    from_core.at[b, at, used],
                    from_y.at[b - 1, at, used],
                    ring_sem.at[turn, 0, n, b - 1],
                    ring_sem.at[turn, 1, n, b - 1],
                    plane_peer[0, b],
                )

        def keep(a, lo, hi, total, extra):
            if extra is None:
                reduced[turn, a, lo:hi] = total
            else:
                reduced[turn, a, lo:hi, 0:4] = total
                reduced[turn, a, lo:hi, 4:8] = jnp.broadcast_to(extra[None], (hi - lo, 4, 128))

        if steps is not None:
            for b in range(1, RING):
                sent["steps", 0, b].wait_recv()
                steps = steps + steps_in[0, b]
        for b in range(1, RING):
            sent["far", b].wait_recv()
        for a in range(CORES):
            total = out[a, 0, rim:depth]
            for b in range(1, RING):
                total = combine(total, from_far[b - 1, a])
            keep(a, rim, depth, total, steps)
        line = {}

        def along(a, slot):
            back = back_of(slot)
            line[a, back] = send(
                reduced.at[turn, a, slot],
                line_in.at[turn, a, back],
                line_sem.at[turn, a, 0, slot],
                line_sem.at[turn, a, 1, back],
                cross_peer[slot] if a else line_peer[offset_of(slot, depth)],
            )

        for slot in range(depth - 1, rim - 1, -1):
            for a in range(CORES):
                along(a, slot)
        if steps is not None:
            for b in range(1, RING):
                sent["steps", 1, b].wait_recv()
                both = both + steps_in[1, b]
            steps = both
        for n in order:
            lo, hi = chunks[n]
            total = from_core[0, lo:hi]
            for b in range(1, RING):
                sent[n, b].wait_recv()
                total = combine(total, from_y[b - 1, lo:hi])
            keep(0, lo, hi, total, steps)
            for slot in range(hi - 1, max(lo, 1) - 1, -1):
                along(0, slot)
        return line

    def collect(turn, line, combine):
        mine = reduced[turn, 0, 0]
        for slot in range(1, depth):
            for a in range(CORES if slot >= rim else 1):
                line[a, slot].wait_recv()
                mine = combine(mine, line_in[turn, a, slot])
        return mine

    def all_gather(turn, block):
        for c in range(COLBLK):
            gathered[turn, 0, 0, c] = block[2 * c : 2 * c + 2]
        line = {}
        for slot in range(depth - 1, 0, -1):
            back = back_of(slot)
            for a in range(CORES if slot >= rim else 1):
                line[a, back] = send(
                    gathered.at[turn, 0, 0, pl.ds(0, COLBLK)],
                    gathered.at[turn, a, 0, pl.ds(back * COLBLK, COLBLK)],
                    back_line_sem.at[turn, a, 0, slot],
                    back_line_sem.at[turn, a, 1, back],
                    cross_peer[slot] if a else line_peer[offset_of(slot, depth)],
                )
        drain(len(line))
        sent = []
        for n, (lo, hi) in enumerate(chunks):
            for slot in range(max(lo, 1), hi):
                line[0, slot].wait_recv()
            at = pl.ds(lo * COLBLK, (hi - lo) * COLBLK)
            for i, (a, b) in enumerate(plane):
                sent.append(
                    send(
                        gathered.at[turn, 0, 0, at],
                        gathered.at[turn, a, (RING - b) % RING, at],
                        back_plane_sem.at[turn, 0, n, i],
                        back_plane_sem.at[turn, 1, n, i],
                        plane_peer[a, b],
                    )
                )
        edge = pl.ds(rim * COLBLK, (depth - rim) * COLBLK)
        for slot in range(rim, depth):
            for a in range(CORES):
                line[a, slot].wait_recv()
        for b in range(1, RING):
            sent.append(
                send(
                    gathered.at[turn, :, 0, edge],
                    gathered.at[turn, :, RING - b, edge],
                    back_far_sem.at[turn, 0, b - 1],
                    back_far_sem.at[turn, 1, b - 1],
                    plane_peer[0, b],
                )
            )
        drain(len(sent))
        for copy in sent:
            copy.wait_recv()

    bits = (depth * COLBLK).bit_length() - 1

    def forward(turn):
        def body(step, acc):
            lhs = []
            for u in range(UNROLL):
                t = step * UNROLL + u
                r = index[0, 0, t]
                at = index[0, 2, t]
                side = at >> (bits + 2)
                pair = gathered[turn, side, (at >> bits) & (RING - 1), at & (depth * COLBLK - 1)]
                value = jnp.where(
                    row < ROWBLK,
                    jnp.broadcast_to(pair[0:1], (8, 128)),
                    jnp.broadcast_to(pair[1:2], (8, 128)),
                )
                lhs.append(split_parts(jnp.where(row % ROWBLK == r, value, 0.0)))
            block = flipped[pl.ds(step * UNROLL, UNROLL)].reshape(UNROLL * 128, 128)
            return acc + jnp.dot(
                jnp.concatenate(lhs, axis=1), block, preferred_element_type=F32
            )

        acc = lax.fori_loop(0, ntile // UNROLL, body, jnp.zeros((16, 128), F32))
        return (acc[0:8] + acc[8:16]) * rscale

    def join(a, b):
        top = lax.broadcasted_iota(jnp.int32, a.shape, a.ndim - 2) < 4
        return jnp.where(top, a + b, jnp.maximum(a, b))

    def add(a, b):
        return a + b

    line = reduce_scatter(0, store_wide, wide_out, wide_core, wide_y, wide_far, join)

    def flip_body(step, carry):
        for u in range(UNROLL):
            t = step * UNROLL + u
            flipped[t] = jnp.transpose(tiles[t])
        return carry

    lax.fori_loop(0, ntile // UNROLL, flip_body, 0)
    mine = collect(0, line, join)

    row4 = lax.broadcasted_iota(jnp.int32, (4, 128), 0)
    cscale = lax.rsqrt(
        jnp.where(
            row4 < 2,
            jnp.broadcast_to(mine[4:5], (4, 128)),
            jnp.broadcast_to(mine[5:6], (4, 128)),
        )
    )
    small[5].wait()
    small[6].wait()
    before = primal_rows(x_start)
    scost = primal_rows(cost) * cscale
    primal = jnp.maximum(0.0, before - step_size * (scost - mine[0:4] * cscale))
    all_gather(0, (2.0 * primal - before) * cscale)
    move = (primal - before) ** 2
    dual = jnp.maximum(0.0, start + step_size * (sbound - forward(0)))
    fill_weights(dual * rscale, table)
    turn = (dual - start) ** 2
    steps = jnp.concatenate(
        [
            move[0:2] + move[2:4],
            jnp.sum(turn[0:4], axis=0, keepdims=True),
            jnp.sum(turn[4:8], axis=0, keepdims=True),
        ],
        axis=0,
    )

    lax.fori_loop(0, ntile // UNROLL, adjoint_body, 0)
    line = reduce_scatter(
        1, store_slim, slim_out, slim_core, slim_y, slim_far, add, steps
    )
    mine = collect(1, line, add)
    sums = jnp.sum(mine[4:8], axis=1, keepdims=True) + 1e-06
    omega = jnp.broadcast_to(jnp.sqrt(sums[2:4] / sums[0:2]), (2, 128))
    wide = jnp.concatenate([omega, omega], axis=0)
    after = jnp.maximum(0.0, primal - (step_size / wide) * (scost - mine[0:4] * cscale))
    all_gather(1, (2.0 * after - primal) * cscale)
    for c in range(COLBLK):
        x_out[:, c * 128 : (c + 1) * 128] = after[2 * c : 2 * c + 2]
    pace = jnp.concatenate(
        [
            jnp.broadcast_to(step_size * omega[0:1], (4, 128)),
            jnp.broadcast_to(step_size * omega[1:2], (4, 128)),
        ],
        axis=0,
    )
    last = jnp.maximum(0.0, dual + pace * (sbound - forward(1)))
    for k in range(2):
        for r in range(ROWBLK):
            y_out[k : k + 1, r * 128 : (r + 1) * 128] = last[k * ROWBLK + r : k * ROWBLK + r + 1]
    drain()


HBM = pl.BlockSpec(memory_space=pltpu.HBM)
VMEM = pl.BlockSpec(memory_space=pltpu.VMEM)
SMEM = pl.BlockSpec(memory_space=pltpu.SMEM)


def shards(tiles, tile_row, tile_col, tile_count, cost, bound_vec, x_start, y_start):
    ntile = tiles.shape[1]
    depth = lax.axis_size("band") // PLANE
    dma = pltpu.SemaphoreType.DMA
    nchunk, rim = (2, depth - 3) if depth >= 8 else (1, 1)
    return pl.pallas_call(
        kernel,
        out_shape=(
            jax.ShapeDtypeStruct((2, COLBLK * 128), F32),
            jax.ShapeDtypeStruct((2, ROWBLK * 128), F32),
        ),
        in_specs=[HBM] * 3 + [SMEM] + [HBM] * 4,
        out_specs=(VMEM, VMEM),
        scratch_shapes=[
            pltpu.VMEM((ntile, 128, 128), BF16),
            pltpu.VMEM((ntile, 128, 128), BF16),
            pltpu.VMEM((ROWBLK + 1, 128, 128), F32),
            pltpu.VMEM((ROWBLK * COLBLK + 1, 16, 128), BF16),
            pltpu.VMEM((ntile + 1, 8, 128), F32),
            pltpu.VMEM((CORES, RING, depth, 8, 128), F32),
            pltpu.VMEM((RING, depth, 8, 128), F32),
            pltpu.VMEM((RING - 1, depth, 8, 128), F32),
            pltpu.VMEM((RING - 1, CORES, depth - rim, 8, 128), F32),
            pltpu.VMEM((CORES, RING, depth, 4, 128), F32),
            pltpu.VMEM((RING, depth, 4, 128), F32),
            pltpu.VMEM((RING - 1, depth, 4, 128), F32),
            pltpu.VMEM((RING - 1, CORES, depth - rim, 4, 128), F32),
            pltpu.VMEM((2, 4, 128), F32),
            pltpu.VMEM((2, RING, 4, 128), F32),
            pltpu.VMEM((2, CORES, depth, 8, 128), F32),
            pltpu.VMEM((2, CORES, depth, 8, 128), F32),
            pltpu.VMEM((2, CORES, RING, depth * COLBLK, 2, 128), F32),
            pltpu.VMEM((1, ntile), jnp.int32),
            pltpu.VMEM((1, ntile), jnp.int32),
            pltpu.VMEM((2, COLBLK * 128), F32),
            pltpu.VMEM((1, ROWBLK * 128), F32),
            pltpu.VMEM((2, COLBLK * 128), F32),
            pltpu.VMEM((2, ROWBLK * 128), F32),
            pltpu.SMEM((1, ntile), jnp.int32),
            pltpu.VMEM((2, 8, 128), jnp.int32),
            pltpu.SMEM((2, 8, 128), jnp.int32),
            dma((ntile // PIECE,)),
            dma((8,)),
            dma((2, 2, nchunk)),
            dma((2, 2, nchunk, RING - 1)),
            dma((2, 2, RING - 1)),
            dma((2, 2, RING)),
            dma((2, CORES, 2, depth)),
            dma((2, CORES, 2, depth)),
            dma((2, 2, nchunk, PLANE - 1)),
            dma((2, 2, RING - 1)),
        ],
        compiler_params=pltpu.CompilerParams(
            collective_id=0, has_side_effects=True, vmem_limit_bytes=60 << 20
        ),
    )(
        tiles,
        tile_row,
        tile_col,
        tile_count,
        cost,
        bound_vec.reshape(1, -1),
        x_start,
        y_start,
    )


def solution(mesh):
    return jax.shard_map(
        shards,
        mesh=mesh,
        in_specs=(
            P("band", None, None, None),
            P("band", None),
            P("band", None),
            P("band"),
            P("batch", "band"),
            P("band"),
            P("batch", "band"),
            P("batch", "band"),
        ),
        out_specs=(P("batch", "band"), P("batch", "band")),
        check_vma=False,
    )
```
